256 devices in a mesh: section: 16 (over x, y_lo, core), dp: 16 (over y_hi, z).
Axes of the slice: x: 4, y: 4 (y_hi: 2, y_lo: 2; y = y_hi * 2 + y_lo), z: 8, core: 2. Of those that a mesh axis runs over, the one named last changes fastest.
Arguments:
- inputs: bfloat16 [16, 2, 4096, 2048], P('section', None, 'dp'), may hold values from -6 to 6
- cotangent: bfloat16 [16, 2, 4096, 2048], P('section', None, 'dp'), may hold values from -6 to 6
- w_gate: bfloat16 [16, 2, 2048, 256], P('section'), may hold values from -0.125 to 0.125
- w_up: bfloat16 [16, 2, 2048, 256], P('section'), may hold values from -0.125 to 0.125
- w_down: bfloat16 [16, 2, 256, 2048], P('section'), may hold values from -0.375 to 0.375
- mom_gate: float32 [16, 2048, 256], P('section', 'dp'), may hold values from -6 to 6
- mom_up: float32 [16, 2048, 256], P('section', 'dp'), may hold values from -6 to 6
- mom_down: float32 [16, 2048, 256], P('section', 'dp'), may hold values from -6 to 6
Outputs:
- grad_in: bfloat16 [16, 2, 4096, 2048], P('section', None, 'dp')
- new_gate: float32 [16, 2048, 256], P('section', 'dp')
- new_up: float32 [16, 2048, 256], P('section', 'dp')
- new_down: float32 [16, 2048, 256], P('section', 'dp')
The draws below stay inside these ranges and needn't reach their ends.
All inputs are finite; a program needn't handle non-finite values.
Results may differ from the reference program's by a relative error of at most 0.009.
Values may be sent and summed in bfloat16 or wider, within the bound.
A program may use at most 128 MiB of HBM per device.

```python
import jax
import jax.numpy as jnp
from jax import lax

D = 2048
FF = 256
TOK_DEV = 256
TOKENS = 4096
N_SECTION = 16
N_DP = 16


def spiked(values, rng, source, target, parts, factor):
    owner, partner = [(jnp.arange(values.shape[axis_at]) // (values.shape[axis_at] // parts)).reshape([-1 if axis == axis_at else 1 for axis in range(values.ndim)]) for axis_at in (source, target)]
    chosen = jax.random.permutation(rng, parts)[partner]
    strong = (owner == chosen) | (owner == (partner + parts // 2) % parts)
    return jnp.where(strong, factor * values, values)


def block_scale(own_key, dims, cuts, least, high):
    factor_of, own = 1.0, jax.random.fold_in(own_key, 6)
    for position, shards_of in cuts:
        steps = jnp.exp(jax.random.uniform(jax.random.fold_in(own, position), (shards_of,), jnp.float32, least / len(cuts), high / len(cuts)))
        factor_of = factor_of * jnp.repeat(steps, dims[position] // shards_of).reshape([-1 if axis == position else 1 for axis in range(len(dims))])
    return factor_of


def gaussian(rng, dims, spread, limit, pieces=(), held_as=jnp.bfloat16):
    drawn = spread * jax.random.normal(rng, dims, jnp.float32)
    if pieces:
        drawn = drawn * block_scale(rng, dims, pieces, -0.22, 0.18)
    return jnp.clip(drawn, -limit, limit).astype(held_as)


def gaussian_with(key, extent, width, bound, pieces, heavy, kind=jnp.bfloat16):
    drawn = width * jax.random.normal(key, extent, jnp.float32)
    if pieces:
        drawn = drawn * block_scale(key, extent, pieces, -0.22, 0.18)
    return jnp.clip(spiked(drawn, jax.random.fold_in(key, 3), *heavy), -bound, bound).astype(kind)


def setup_inputs(seed: int = 0) -> dict:
    streams_of = jax.random.split(jax.random.key(seed), 9)
    inputs = gaussian_with(streams_of[0], (N_SECTION, 2, TOKENS, D), 1.0, 6.0, ((0, 16), (2, 16)), (2, 3, 16, 2.0))
    cotangent = gaussian_with(streams_of[1], (N_SECTION, 2, TOKENS, D), 1.0, 6.0, ((0, 16), (2, 16)), (2, 3, 16, 2.0))
    w_gate = gaussian(streams_of[2], (N_SECTION, 2, D, FF), D ** -0.5, 0.125, ((0, 16),))
    w_up = gaussian(streams_of[3], (N_SECTION, 2, D, FF), D ** -0.5, 0.125, ((0, 16),))
    w_down = gaussian(streams_of[4], (N_SECTION, 2, FF, D), FF ** -0.5, 0.375, ((0, 16),))
    mom_gate = gaussian(streams_of[5], (N_SECTION, D, FF), 1.0, 6.0, ((0, 16), (1, 16)), jnp.float32)
    mom_up = gaussian(streams_of[6], (N_SECTION, D, FF), 1.0, 6.0, ((0, 16), (1, 16)), jnp.float32)
    mom_down = gaussian(streams_of[7], (N_SECTION, D, FF), 1.0, 6.0, ((0, 16), (1, 16)), jnp.float32)
    return dict(inputs=inputs, cotangent=cotangent, w_gate=w_gate, w_up=w_up, w_down=w_down, mom_gate=mom_gate, mom_up=mom_up, mom_down=mom_down)


def backward_block(block_in, block_cot, gate_mat, up_mat, down_mat):
    gate_pre = jnp.dot(block_in, gate_mat, preferred_element_type=jnp.float32)
    up_pre = jnp.dot(block_in, up_mat, preferred_element_type=jnp.float32)
    sigmoid_val = jax.nn.sigmoid(gate_pre)
    activated = gate_pre * sigmoid_val
    hidden = (activated * up_pre).astype(jnp.bfloat16)
    hidden_grad = jnp.dot(block_cot, down_mat.T, preferred_element_type=jnp.float32)
    gate_grad = (hidden_grad * up_pre * sigmoid_val * (1.0 + gate_pre * (1.0 - sigmoid_val))).astype(jnp.bfloat16)
    up_grad = (hidden_grad * activated).astype(jnp.bfloat16)
    input_grad = (jnp.dot(gate_grad, gate_mat.T, preferred_element_type=jnp.float32) + jnp.dot(up_grad, up_mat.T, preferred_element_type=jnp.float32)).astype(jnp.bfloat16)
    return (input_grad, gate_grad, up_grad, hidden)

def replica_grads(block_in, block_cot, gate_grad, up_grad, hidden):
    groups_in = block_in.reshape(N_DP, TOK_DEV, D).astype(jnp.float32)
    groups_cot = block_cot.reshape(N_DP, TOK_DEV, D).astype(jnp.float32)
    groups_gate = gate_grad.reshape(N_DP, TOK_DEV, FF).astype(jnp.float32)
    groups_up = up_grad.reshape(N_DP, TOK_DEV, FF).astype(jnp.float32)
    groups_hid = hidden.reshape(N_DP, TOK_DEV, FF).astype(jnp.float32)
    part_gate = jnp.einsum('gtd,gtf->gdf', groups_in, groups_gate)
    part_up = jnp.einsum('gtd,gtf->gdf', groups_in, groups_up)
    part_down = jnp.einsum('gtd,gtf->gdf', groups_cot, groups_hid)
    return jnp.stack([part_gate, part_up, part_down])

def per_section(packed):
    section_in, section_cot, section_gate, section_up, section_down = packed
    first = backward_block(section_in[0], section_cot[0], section_gate[0], section_up[0], section_down[0])
    second = backward_block(section_in[1], section_cot[1], section_gate[1], section_up[1], section_down[1])
    parts_first = replica_grads(section_in[0], section_cot[0], first[1], first[2], first[3])
    parts_second = replica_grads(section_in[1], section_cot[1], second[1], second[2], second[3])
    rounded = lax.optimization_barrier(parts_second.astype(jnp.bfloat16)).astype(jnp.float32)
    return (jnp.stack([first[0], second[0]]), lax.optimization_barrier(jnp.sum(parts_first, axis=1)), lax.optimization_barrier(jnp.sum(rounded, axis=1)))

def reference(inputs, cotangent, w_gate, w_up, w_down, mom_gate, mom_up, mom_down):
    input_grads, grads_first, grads_second = lax.map(per_section, (inputs, cotangent, w_gate, w_up, w_down))
    zero_rows = jnp.zeros((1, TOKENS, D), jnp.bfloat16)
    recv_first = jnp.concatenate([input_grads[1:, 0], zero_rows], axis=0)
    recv_second = jnp.concatenate([zero_rows, input_grads[:-1, 1]], axis=0)
    grad_in = jnp.stack([recv_first, recv_second], axis=1)
    combined = grads_first + jnp.flip(grads_second, axis=0)
    scale_factor = 1.0 / jnp.sqrt(jnp.float32(TOKENS))
    new_gate = 0.9 * mom_gate + combined[:, 0] * scale_factor
    new_up = 0.9 * mom_up + combined[:, 1] * scale_factor
    new_down = 0.9 * mom_down + combined[:, 2] * scale_factor
    return (grad_in, new_gate, new_up, new_down)
```

```python
import functools

import jax
import jax.numpy as jnp
from jax import lax
from jax.experimental import pallas as pl
from jax.experimental.pallas import tpu as pltpu
from jax.sharding import PartitionSpec as P

MESH = pl.DeviceIdType.MESH
NH = 2
BF16 = jnp.bfloat16
F32 = jnp.float32


def kernel(
    ns, nz, tok, dim, ff,
    x_hbm, y_hbm, wg_hbm, wu_hbm, wd_hbm, mg_ref, mu_ref, md_ref,
    gin, ng_ref, nu_ref, nd_ref,
    xb, yb, wgb, wub, wdb, act, act_t, pre, part, ring, dxb, out1, late,
    in_sem, ring_send, ring_recv, dx_send, dx_recv, zero_sem, late_send, late_recv,
):
    sec = lax.axis_index("section")
    dp = lax.axis_index("dp")
    half = dp // nz
    z = dp % nz
    width = dim // (NH * nz)
    three = 3 * ff
    far = nz // 2
    mirror = ns - 1 - sec
    total_rows = tok * NH * nz

    def at_z(distance):
        return (z + distance + nz) % nz

    def device(s, h, zz):
        return (s, h * nz + zz)

    loads = []
    for b in (1, 0):
        for n, (src, dst) in enumerate(
            ((x_hbm, xb), (wg_hbm, wgb), (wu_hbm, wub), (y_hbm, yb), (wd_hbm, wdb))
        ):
            copy = pltpu.make_async_copy(src.at[0, b], dst.at[b], in_sem.at[b, n])
            copy.start()
            loads.append(copy)

    def load(b, n, src, dst):
        return pltpu.make_async_copy(src.at[0, b], dst.at[b], in_sem.at[b, n])

    barrier = pltpu.get_barrier_semaphore()
    neighbours = [
        device(sec, half, at_z(1)),
        device(sec, half, at_z(-1)),
        device(mirror, 0, z),
        device(mirror, 1, z),
        device(sec, 1 - half, z),
        device((sec + 1) % ns, half, z),
        device((sec + ns - 1) % ns, half, z),
    ]
    for target in neighbours:
        pl.semaphore_signal(barrier, inc=1, device_id=target, device_id_type=MESH)

    def forward(i, carry):
        b = 1 - i
        load(b, 0, x_hbm, xb).wait()
        load(b, 1, wg_hbm, wgb).wait()
        pre[0] = jnp.dot(xb[b], wgb[b], preferred_element_type=F32)
        load(b, 2, wu_hbm, wub).wait()
        pre[1] = jnp.dot(xb[b], wub[b], preferred_element_type=F32)
        load(b, 3, y_hbm, yb).wait()
        load(b, 4, wd_hbm, wdb).wait()
        pre[2] = lax.dot_general(
            yb[b], wdb[b], (((1,), (1,)), ((), ())), preferred_element_type=F32
        )
        step = min(128, tok)
        for row in range(0, tok, step):
            rows = pl.ds(row, step)
            gpre, upre, dhid = pre[0, rows, :], pre[1, rows, :], pre[2, rows, :]
            sig = jax.nn.sigmoid(gpre)
            activated = gpre * sig
            dgate = dhid * upre * sig * (1.0 + gpre * (1.0 - sig))
            dup = dhid * activated
            hidden = activated * upre
            act[b, 0, rows, :] = dgate.astype(BF16)
            act[b, 1, rows, :] = dup.astype(BF16)
            act_t[b, 0:ff, rows] = dgate.T.astype(BF16)
            act_t[b, ff : 2 * ff, rows] = dup.T.astype(BF16)
            act_t[b, 2 * ff : three, rows] = hidden.T.astype(BF16)
        return carry

    def weight_grad(b, h, pair):
        start = pl.multiple_of((h * nz + 2 * pair) * width, 2 * width)
        cols = pl.ds(start, 2 * width)
        gate_up = jnp.dot(act_t[b, 0 : 2 * ff, :], xb[b, :, cols], preferred_element_type=F32)
        part[b, h, 2 * pair, 0 : 2 * ff, :] = gate_up[:, :width].astype(BF16)
        part[b, h, 2 * pair + 1, 0 : 2 * ff, :] = gate_up[:, width:].astype(BF16)
        down = jnp.dot(act_t[b, 2 * ff : three, :], yb[b, :, cols], preferred_element_type=F32)
        part[b, h, 2 * pair, 2 * ff : three, :] = down[:, :width].astype(BF16)
        part[b, h, 2 * pair + 1, 2 * ff : three, :] = down[:, width:].astype(BF16)

    def message(direction, h, d, b):
        sign = -1 if direction == 0 else 1
        return pltpu.make_async_remote_copy(
            src_ref=part.at[b, h, at_z(sign * d)],
            dst_ref=ring.at[direction, h, d - 1, b],
            send_sem=ring_send.at[direction, h, d - 1, b],
            recv_sem=ring_recv.at[direction, h, d - 1, b],
            device_id=device(sec, half, at_z(sign)),
            device_id_type=MESH,
        )

    def accumulate(direction, h, d, b):
        sign = -1 if direction == 0 else 1
        message(direction, h, d + 1, b).wait_recv()
        target = at_z(sign * d)
        mine = part[b, h, target].astype(F32)
        part[b, h, target] = (mine + ring[direction, h, d, b].astype(F32)).astype(BF16)

    long = ((0, 0), (1, 1))
    short = ((0, 1), (1, 0))

    half_z = z // 2
    pairs = nz // 2
    first_pair = (half_z + far // 2) % pairs

    for i in range(2):
        b = 1 - i
        forward(i, 0)
        for h in range(NH):
            weight_grad(b, h, first_pair)
        if i == 0:
            pl.semaphore_wait(barrier, len(neighbours))
        for direction, h in long:
            message(direction, h, far, b).start()

    def rest(j, carry):
        pair = (half_z + far // 2 + 1 + j) % pairs
        for b in (1, 0):
            for h in range(NH):
                weight_grad(b, h, pair)
        return carry

    lax.fori_loop(0, pairs - 1, rest, 0)
    if far > 1:
        for b in (1, 0):
            for direction, h in short:
                message(direction, h, far - 1, b).start()

    def dx_copy(b):
        step = -1 if b == 0 else 1
        return pltpu.make_async_remote_copy(
            src_ref=dxb.at[b],
            dst_ref=gin.at[0, b],
            send_sem=dx_send.at[b],
            recv_sem=dx_recv.at[b],
            device_id=device(sec + step, half, z),
            device_id_type=MESH,
        )

    def zero_copy(b):
        return pltpu.make_async_copy(dxb.at[b], gin.at[0, 1 - b], zero_sem)

    cut = 2 * width
    for b in (1, 0):

        def dx_chunk(j, carry, b=b):
            cols = pl.ds(pl.multiple_of(j * cut, cut), cut)
            contract = (((1,), (1,)), ((), ()))
            dx = lax.dot_general(
                act[b, 0], wgb[b, cols, :], contract, preferred_element_type=F32
            ) + lax.dot_general(act[b, 1], wub[b, cols, :], contract, preferred_element_type=F32)
            dxb[b, :, cols] = dx.astype(BF16)
            return carry

        sends = sec > 0 if b == 0 else sec < ns - 1

        @pl.when(sends)
        def _(b=b, dx_chunk=dx_chunk):
            lax.fori_loop(0, dim // cut, dx_chunk, 0)
            dx_copy(b).start()

        @pl.when(jnp.logical_not(sends))
        def _(b=b):
            dxb[b] = jnp.zeros((tok, dim), BF16)
            zero_copy(b).start()

    for d in range(far - 1, 0, -1):
        for b in (1, 0):
            for direction, h in long:
                accumulate(direction, h, d, b)
                message(direction, h, d, b).start()
        if d > 1:
            for b in (1, 0):
                for direction, h in short:
                    accumulate(direction, h, d - 1, b)
                    message(direction, h, d - 1, b).start()

    def reduced(b, h):
        return (
            part[b, h, z].astype(F32)
            + ring[0, h, 0, b].astype(F32)
            + ring[1, h, 0, b].astype(F32)
        )

    def finish_wait(b, h):
        message(0, h, 1, b).wait_recv()
        message(1, h, 1, b).wait_recv()

    def late_copy(n):
        if n < NH:
            target, slot = device(mirror, n, z), half
        else:
            target, slot = device(sec, 1 - half, z), NH
        return pltpu.make_async_remote_copy(
            src_ref=out1.at[n],
            dst_ref=late.at[slot],
            send_sem=late_send.at[n],
            recv_sem=late_recv.at[slot],
            device_id=target,
            device_id_type=MESH,
        )

    for h in range(NH):
        finish_wait(1, h)
        out1[h] = reduced(1, h).astype(BF16)
        late_copy(h).start()
    for h in range(NH):
        finish_wait(0, h)
    out1[NH] = reduced(0, 1 - half).astype(BF16)
    late_copy(NH).start()

    def late_wait(slot):
        pltpu.make_async_remote_copy(
            src_ref=out1.at[0],
            dst_ref=late.at[slot],
            send_sem=late_send.at[0],
            recv_sem=late_recv.at[slot],
            device_id=device(mirror, 0, z),
            device_id_type=MESH,
        ).wait_recv()

    for slot in range(3):
        late_wait(slot)
    scale = 1.0 / float(total_rows) ** 0.5
    for n, (mom, new) in enumerate(((mg_ref, ng_ref), (mu_ref, nu_ref), (md_ref, nd_ref))):
        rows = pl.ds(n * ff, ff)
        total = (
            part[0, half, z, rows, :].astype(F32)
            + ring[0, half, 0, 0, rows, :].astype(F32)
            + ring[1, half, 0, 0, rows, :].astype(F32)
        )
        for slot in range(3):
            total = total + late[slot, rows, :].astype(F32)
        new[0] = 0.9 * mom[0] + total.T * scale

    for h in range(NH):
        late_copy(h).wait_send()
    late_copy(NH).wait_send()
    for b in range(2):
        for d in range(1, far + 1):
            for direction, h in long + (short if d < far else ()):
                message(direction, h, d, b).wait_send()

    @pl.when(sec > 0)
    def _():
        dx_copy(0).wait_send()
        dx_copy(1).wait_recv()

    @pl.when(sec < ns - 1)
    def _():
        dx_copy(1).wait_send()
        dx_copy(0).wait_recv()

    @pl.when(sec == 0)
    def _():
        zero_copy(0).wait()

    @pl.when(sec == ns - 1)
    def _():
        zero_copy(1).wait()


def body(inputs, cotangent, w_gate, w_up, w_down, mom_gate, mom_up, mom_down):
    ns = lax.axis_size("section")
    nz = lax.axis_size("dp") // NH
    _, _, tok, dim = inputs.shape
    ff = w_gate.shape[-1]
    far = nz // 2
    width = dim // (NH * nz)
    anywhere = pl.BlockSpec(memory_space=pl.ANY)
    vmem = pl.BlockSpec(memory_space=pltpu.VMEM)
    dma = pltpu.SemaphoreType.DMA
    return pl.pallas_call(
        functools.partial(kernel, ns, nz, tok, dim, ff),
        out_shape=(
            jax.ShapeDtypeStruct(inputs.shape, BF16),
            jax.ShapeDtypeStruct(mom_gate.shape, F32),
            jax.ShapeDtypeStruct(mom_up.shape, F32),
            jax.ShapeDtypeStruct(mom_down.shape, F32),
        ),
        in_specs=[anywhere] * 5 + [vmem] * 3,
        out_specs=(anywhere, vmem, vmem, vmem),
        scratch_shapes=[
            pltpu.VMEM((2, tok, dim), BF16),
            pltpu.VMEM((2, tok, dim), BF16),
            pltpu.VMEM((2, dim, ff), BF16),
            pltpu.VMEM((2, dim, ff), BF16),
            pltpu.VMEM((2, ff, dim), BF16),
            pltpu.VMEM((2, 2, tok, ff), BF16),
            pltpu.VMEM((2, 3 * ff, tok), BF16),
            pltpu.VMEM((3, tok, ff), F32),
            pltpu.VMEM((2, NH, nz, 3 * ff, width), BF16),
            pltpu.VMEM((2, NH, far, 2, 3 * ff, width), BF16),
            pltpu.VMEM((2, tok, dim), BF16),
            pltpu.VMEM((NH + 1, 3 * ff, width), BF16),
            pltpu.VMEM((3, 3 * ff, width), BF16),
            dma((2, 5)),
            dma((2, NH, far, 2)),
            dma((2, NH, far, 2)),
            dma((2,)),
            dma((2,)),
            dma,
            dma((NH + 1,)),
            dma((3,)),
        ],
        compiler_params=pltpu.CompilerParams(
            collective_id=0, has_side_effects=True, vmem_limit_bytes=56 * 2**20
        ),
        name="relay_step",
    )(inputs, cotangent, w_gate, w_up, w_down, mom_gate, mom_up, mom_down)


def solution(mesh):
    placed = (
        P("section", None, "dp", None),
        P("section", None, "dp", None),
        P("section", None, None, None),
        P("section", None, None, None),
        P("section", None, None, None),
        P("section", "dp", None),
        P("section", "dp", None),
        P("section", "dp", None),
    )
    return jax.shard_map(
        body,
        mesh=mesh,
        in_specs=placed,
        out_specs=(
            P("section", None, "dp", None),
            P("section", "dp", None),
            P("section", "dp", None),
            P("section", "dp", None),
        ),
        check_vma=False,
    )
```

```python
import functools

import jax
import jax.numpy as jnp
from jax import lax
from jax.experimental import pallas as pl
from jax.experimental.pallas import tpu as pltpu
from jax.sharding import PartitionSpec as P

MESH = pl.DeviceIdType.MESH
NH = 2
CROSS = 0.25
BF16 = jnp.bfloat16
F32 = jnp.float32


def kernel(
    ns, nz, tok, dim, ff, cross,
    x_hbm, y_hbm, wg_hbm, wu_hbm, wd_hbm, mg_ref, mu_ref, md_ref,
    gin, ng_ref, nu_ref, nd_ref,
    xb, yb, wgb, wub, wdb, act, act_t, pre, part, ring, dxb, out1, late,
    wide, wide_in, wide_ring,
    in_sem, ring_send, ring_recv, dx_send, dx_recv, zero_sem, late_send, late_recv,
    wide_send, wide_recv, wide_ring_send, wide_ring_recv,
):
    sec = lax.axis_index("section")
    dp = lax.axis_index("dp")
    half = dp // nz
    z = dp % nz
    width = dim // (NH * nz)
    three = 3 * ff
    keep = three - cross
    far = nz // 2
    mirror = ns - 1 - sec
    total_rows = tok * NH * nz

    def at_z(distance):
        return (z + distance + nz) % nz

    def device(s, h, zz):
        return (s, h * nz + zz)

    loads = []
    for b in (1, 0):
        for n, (src, dst) in enumerate(
            ((x_hbm, xb), (wg_hbm, wgb), (wu_hbm, wub), (y_hbm, yb), (wd_hbm, wdb))
        ):
            copy = pltpu.make_async_copy(src.at[0, b], dst.at[b], in_sem.at[b, n])
            copy.start()
            loads.append(copy)

    def load(b, n, src, dst):
        return pltpu.make_async_copy(src.at[0, b], dst.at[b], in_sem.at[b, n])

    barrier = pltpu.get_barrier_semaphore()
    neighbours = [
        device(sec, half, at_z(1)),
        device(sec, half, at_z(-1)),
        device(mirror, 0, z),
        device(mirror, 1, z),
        device(sec, 1 - half, z),
        device((sec + 1) % ns, half, z),
        device((sec + ns - 1) % ns, half, z),
    ]
    for target in neighbours:
        pl.semaphore_signal(barrier, inc=1, device_id=target, device_id_type=MESH)

    def forward(i, carry):
        b = 1 - i
        load(b, 0, x_hbm, xb).wait()
        load(b, 1, wg_hbm, wgb).wait()
        pre[0] = jnp.dot(xb[b], wgb[b], preferred_element_type=F32)
        load(b, 2, wu_hbm, wub).wait()
        pre[1] = jnp.dot(xb[b], wub[b], preferred_element_type=F32)
        load(b, 3, y_hbm, yb).wait()
        load(b, 4, wd_hbm, wdb).wait()
        pre[2] = lax.dot_general(
            yb[b], wdb[b], (((1,), (1,)), ((), ())), preferred_element_type=F32
        )
        step = min(128, tok)
        for row in range(0, tok, step):
            rows = pl.ds(row, step)
            gpre, upre, dhid = pre[0, rows, :], pre[1, rows, :], pre[2, rows, :]
            sig = jax.nn.sigmoid(gpre)
            activated = gpre * sig
            dgate = dhid * upre * sig * (1.0 + gpre * (1.0 - sig))
            dup = dhid * activated
            hidden = activated * upre
            act[b, 0, rows, :] = dgate.astype(BF16)
            act[b, 1, rows, :] = dup.astype(BF16)
            act_t[b, 0:ff, rows] = dgate.T.astype(BF16)
            act_t[b, ff : 2 * ff, rows] = dup.T.astype(BF16)
            act_t[b, 2 * ff : three, rows] = hidden.T.astype(BF16)
        return carry

    def weight_grad(b, h, pair):
        start = pl.multiple_of((h * nz + 2 * pair) * width, 2 * width)
        cols = pl.ds(start, 2 * width)
        gate_up = jnp.dot(act_t[b, 0 : 2 * ff, :], xb[b, :, cols], preferred_element_type=F32)
        part[b, h, 2 * pair, 0 : 2 * ff, :] = gate_up[:, :width].astype(BF16)
        part[b, h, 2 * pair + 1, 0 : 2 * ff, :] = gate_up[:, width:].astype(BF16)
        down = jnp.dot(act_t[b, 2 * ff : three, :], yb[b, :, cols], preferred_element_type=F32)
        for n in range(2):
            tile = down[:, n * width : (n + 1) * width].astype(BF16)
            if keep > 2 * ff:
                part[b, h, 2 * pair + n, 2 * ff : keep, :] = tile[: keep - 2 * ff]
            wide[b, h, 2 * pair + n] = tile[keep - 2 * ff :]

    def wide_copy(n):
        if n < NH:
            src, target, slot = wide.at[1, n], device(mirror, n, z), half
        else:
            src, target, slot = wide.at[0, 1 - half], device(sec, 1 - half, z), NH
        return pltpu.make_async_remote_copy(
            src_ref=src,
            dst_ref=wide_in.at[slot],
            send_sem=wide_send.at[n],
            recv_sem=wide_recv.at[slot],
            device_id=target,
            device_id_type=MESH,
        )

    def wide_wait(slot):
        pltpu.make_async_remote_copy(
            src_ref=wide.at[1, 0],
            dst_ref=wide_in.at[slot],
            send_sem=wide_send.at[0],
            recv_sem=wide_recv.at[slot],
            device_id=device(mirror, 0, z),
            device_id_type=MESH,
        ).wait_recv()

    part_rows = cross // 2

    def wide_message(direction, g, d):
        sign = -1 if direction == 0 else 1
        return pltpu.make_async_remote_copy(
            src_ref=wide.at[0, half, at_z(sign * d), pl.ds(g * part_rows, part_rows)],
            dst_ref=wide_ring.at[direction, g, d - 1],
            send_sem=wide_ring_send.at[direction, g, d - 1],
            recv_sem=wide_ring_recv.at[direction, g, d - 1],
            device_id=device(sec, half, at_z(sign)),
            device_id_type=MESH,
        )

    def wide_sum(target):
        total = wide[0, half, target].astype(F32)
        for slot in range(NH + 1):
            total = total + wide_in[slot, target].astype(F32)
        wide[0, half, target] = total.astype(BF16)

    def wide_accumulate(direction, g, d):
        sign = -1 if direction == 0 else 1
        wide_message(direction, g, d + 1).wait_recv()
        target = at_z(sign * d)
        rows = pl.ds(g * part_rows, part_rows)
        mine = wide[0, half, target, rows, :].astype(F32)
        wide[0, half, target, rows, :] = (mine + wide_ring[direction, g, d].astype(F32)).astype(BF16)

    def message(direction, h, d, b):
        sign = -1 if direction == 0 else 1
        return pltpu.make_async_remote_copy(
            src_ref=part.at[b, h, at_z(sign * d)],
            dst_ref=ring.at[direction, h, d - 1, b],
            send_sem=ring_send.at[direction, h, d - 1, b],
            recv_sem=ring_recv.at[direction, h, d - 1, b],
            device_id=device(sec, half, at_z(sign)),
            device_id_type=MESH,
        )

    def accumulate(direction, h, d, b):
        sign = -1 if direction == 0 else 1
        message(direction, h, d + 1, b).wait_recv()
        target = at_z(sign * d)
        mine = part[b, h, target].astype(F32)
        part[b, h, target] = (mine + ring[direction, h, d, b].astype(F32)).astype(BF16)

    long = ((0, 0), (1, 1))
    short = ((0, 1), (1, 0))

    half_z = z // 2
    pairs = nz // 2
    first_pair = (half_z + far // 2) % pairs

    for i in range(2):
        b = 1 - i
        forward(i, 0)
        for h in range(NH):
            weight_grad(b, h, first_pair)
        if i == 0:
            pl.semaphore_wait(barrier, len(neighbours))
        for direction, h in long:
            message(direction, h, far, b).start()

        def rest(j, carry, b=b):
            pair = (half_z + far // 2 + 1 + j) % pairs
            for h in range(NH):
                weight_grad(b, h, pair)
            return carry

        lax.fori_loop(0, pairs - 1, rest, 0)
        if b == 1:
            wide_copy(0).start()
            wide_copy(1).start()
        else:
            wide_copy(NH).start()
        if far > 1:
            for direction, h in short:
                message(direction, h, far - 1, b).start()

    def dx_copy(b):
        step = -1 if b == 0 else 1
        return pltpu.make_async_remote_copy(
            src_ref=dxb.at[b],
            dst_ref=gin.at[0, b],
            send_sem=dx_send.at[b],
            recv_sem=dx_recv.at[b],
            device_id=device(sec + step, half, z),
            device_id_type=MESH,
        )

    def zero_copy(b):
        return pltpu.make_async_copy(dxb.at[b], gin.at[0, 1 - b], zero_sem)

    cut = 2 * width
    for b in (1, 0):

        def dx_chunk(j, carry, b=b):
            cols = pl.ds(pl.multiple_of(j * cut, cut), cut)
            contract = (((1,), (1,)), ((), ()))
            dx = lax.dot_general(
                act[b, 0], wgb[b, cols, :], contract, preferred_element_type=F32
            ) + lax.dot_general(act[b, 1], wub[b, cols, :], contract, preferred_element_type=F32)
            dxb[b, :, cols] = dx.astype(BF16)
            return carry

        sends = sec > 0 if b == 0 else sec < ns - 1

        @pl.when(sends)
        def _(b=b, dx_chunk=dx_chunk):
            lax.fori_loop(0, dim // cut, dx_chunk, 0)
            dx_copy(b).start()

        @pl.when(jnp.logical_not(sends))
        def _(b=b):
            dxb[b] = jnp.zeros((tok, dim), BF16)
            zero_copy(b).start()

    def ring_step(lanes, d):
        for b in (1, 0):
            for direction, h in lanes:
                accumulate(direction, h, d, b)
                message(direction, h, d, b).start()

    def wide_start():
        for slot in range(NH + 1):
            wide_wait(slot)
        for d in range(far, -1, -1):
            for sign in (-1, 1) if 0 < d < far else (1,):
                wide_sum(at_z(sign * d))
            if d == far:
                for direction, g in long:
                    wide_message(direction, g, far).start()
            elif d == far - 1 and d > 0:
                for direction, g in short:
                    wide_message(direction, g, d).start()

    def wide_step(lanes, d):
        for direction, g in lanes:
            wide_accumulate(direction, g, d)
            wide_message(direction, g, d).start()

    for d in range(far - 1, 0, -1):
        if d == 1:
            wide_start()
        ring_step(long, d)
        if d > 1:
            ring_step(short, d - 1)
    for d in range(far - 1, 0, -1):
        wide_step(long, d)
        if d > 1:
            wide_step(short, d - 1)

    def reduced(b, h):
        return (
            part[b, h, z].astype(F32)
            + ring[0, h, 0, b].astype(F32)
            + ring[1, h, 0, b].astype(F32)
        )

    def finish_wait(b, h):
        message(0, h, 1, b).wait_recv()
        message(1, h, 1, b).wait_recv()

    def late_copy(n):
        if n < NH:
            target, slot = device(mirror, n, z), half
        else:
            target, slot = device(sec, 1 - half, z), NH
        return pltpu.make_async_remote_copy(
            src_ref=out1.at[n],
            dst_ref=late.at[slot],
            send_sem=late_send.at[n],
            recv_sem=late_recv.at[slot],
            device_id=target,
            device_id_type=MESH,
        )

    for h in range(NH):
        finish_wait(1, h)
        out1[h] = reduced(1, h).astype(BF16)
        late_copy(h).start()
    for h in range(NH):
        finish_wait(0, h)
    out1[NH] = reduced(0, 1 - half).astype(BF16)
    late_copy(NH).start()

    def late_wait(slot):
        pltpu.make_async_remote_copy(
            src_ref=out1.at[0],
            dst_ref=late.at[slot],
            send_sem=late_send.at[0],
            recv_sem=late_recv.at[slot],
            device_id=device(mirror, 0, z),
            device_id_type=MESH,
        ).wait_recv()

    for slot in range(3):
        late_wait(slot)
    scale = 1.0 / float(total_rows) ** 0.5
    for direction in range(2):
        for g in range(2):
            wide_message(direction, g, 1).wait_recv()

    def total_of(lo, hi):
        rows = pl.ds(lo, hi - lo)
        total = (
            part[0, half, z, rows, :].astype(F32)
            + ring[0, half, 0, 0, rows, :].astype(F32)
            + ring[1, half, 0, 0, rows, :].astype(F32)
        )
        for slot in range(3):
            total = total + late[slot, rows, :].astype(F32)
        return total

    pieces = [total_of(2 * ff, keep)] if keep > 2 * ff else []
    for g in range(2):
        rows = pl.ds(g * part_rows, part_rows)
        pieces.append(
            wide[0, half, z, rows, :].astype(F32)
            + wide_ring[0, g, 0].astype(F32)
            + wide_ring[1, g, 0].astype(F32)
        )
    totals = (total_of(0, ff), total_of(ff, 2 * ff), jnp.concatenate(pieces, axis=0))
    for total, mom, new in zip(totals, (mg_ref, mu_ref, md_ref), (ng_ref, nu_ref, nd_ref)):
        new[0] = 0.9 * mom[0] + total.T * scale

    for h in range(NH):
        late_copy(h).wait_send()
    late_copy(NH).wait_send()
    for n in range(NH + 1):
        wide_copy(n).wait_send()
    for d in range(1, far + 1):
        for direction, g in long + (short if d < far else ()):
            wide_message(direction, g, d).wait_send()
    for b in range(2):
        for d in range(1, far + 1):
            for direction, h in long + (short if d < far else ()):
                message(direction, h, d, b).wait_send()

    @pl.when(sec > 0)
    def _():
        dx_copy(0).wait_send()
        dx_copy(1).wait_recv()

    @pl.when(sec < ns - 1)
    def _():
        dx_copy(1).wait_send()
        dx_copy(0).wait_recv()

    @pl.when(sec == 0)
    def _():
        zero_copy(0).wait()

    @pl.when(sec == ns - 1)
    def _():
        zero_copy(1).wait()


def body(inputs, cotangent, w_gate, w_up, w_down, mom_gate, mom_up, mom_down):
    ns = lax.axis_size("section")
    nz = lax.axis_size("dp") // NH
    _, _, tok, dim = inputs.shape
    ff = w_gate.shape[-1]
    far = nz // 2
    width = dim // (NH * nz)
    cross = int(3 * ff * CROSS) // 32 * 32
    keep = 3 * ff - cross
    anywhere = pl.BlockSpec(memory_space=pl.ANY)
    vmem = pl.BlockSpec(memory_space=pltpu.VMEM)
    dma = pltpu.SemaphoreType.DMA
    return pl.pallas_call(
        functools.partial(kernel, ns, nz, tok, dim, ff, cross),
        out_shape=(
            jax.ShapeDtypeStruct(inputs.shape, BF16),
            jax.ShapeDtypeStruct(mom_gate.shape, F32),
            jax.ShapeDtypeStruct(mom_up.shape, F32),
            jax.ShapeDtypeStruct(mom_down.shape, F32),
        ),
        in_specs=[anywhere] * 5 + [vmem] * 3,
        out_specs=(anywhere, vmem, vmem, vmem),
        scratch_shapes=[
            pltpu.VMEM((2, tok, dim), BF16),
            pltpu.VMEM((2, tok, dim), BF16),
            pltpu.VMEM((2, dim, ff), BF16),
            pltpu.VMEM((2, dim, ff), BF16),
            pltpu.VMEM((2, ff, dim), BF16),
            pltpu.VMEM((2, 2, tok, ff), BF16),
            pltpu.VMEM((2, 3 * ff, tok), BF16),
            pltpu.VMEM((3, tok, ff), F32),
            pltpu.VMEM((2, NH, nz, keep, width), BF16),
            pltpu.VMEM((2, NH, far, 2, keep, width), BF16),
            pltpu.VMEM((2, tok, dim), BF16),
            pltpu.VMEM((NH + 1, keep, width), BF16),
            pltpu.VMEM((NH + 1, keep, width), BF16),
            pltpu.VMEM((2, NH, nz, cross, width), BF16),
            pltpu.VMEM((NH + 1, nz, cross, width), BF16),
            pltpu.VMEM((2, 2, far, cross // 2, width), BF16),
            dma((2, 5)),
            dma((2, NH, far, 2)),
            dma((2, NH, far, 2)),
            dma((2,)),
            dma((2,)),
            dma,
            dma((NH + 1,)),
            dma((NH + 1,)),
            dma((NH + 1,)),
            dma((NH + 1,)),
            dma((2, 2, far)),
            dma((2, 2, far)),
        ],
        compiler_params=pltpu.CompilerParams(
            collective_id=0, has_side_effects=True, vmem_limit_bytes=56 * 2**20
        ),
        name="relay_step",
    )(inputs, cotangent, w_gate, w_up, w_down, mom_gate, mom_up, mom_down)


def solution(mesh):
    placed = (
        P("section", None, "dp", None),
        P("section", None, "dp", None),
        P("section", None, None, None),
        P("section", None, None, None),
        P("section", None, None, None),
        P("section", "dp", None),
        P("section", "dp", None),
        P("section", "dp", None),
    )
    return jax.shard_map(
        body,
        mesh=mesh,
        in_specs=placed,
        out_specs=(
            P("section", None, "dp", None),
            P("section", "dp", None),
            P("section", "dp", None),
            P("section", "dp", None),
        ),
        check_vma=False,
    )
```

```python
import functools

import jax
import jax.numpy as jnp
from jax import lax
from jax.experimental import pallas as pl
from jax.experimental.pallas import tpu as pltpu
from jax.sharding import PartitionSpec as P

MESH = pl.DeviceIdType.MESH
NH = 2
CROSS = 0.25
BF16 = jnp.bfloat16
F32 = jnp.float32


def kernel(
    ns, nz, tok, dim, ff, cross,
    x_hbm, y_hbm, wg_hbm, wu_hbm, wd_hbm,
    gin, total_ref,
    xb, yb, wgb, wub, wdb, act, act_t, pre, part, ring, dxb, out1, late,
    wide, wide_in, wide_ring,
    in_sem, ring_send, ring_recv, dx_send, dx_recv, zero_sem, late_send, late_recv,
    wide_send, wide_recv, wide_ring_send, wide_ring_recv,
):
    sec = lax.axis_index("section")
    dp = lax.axis_index("dp")
    half = dp // nz
    z = dp % nz
    width = dim // (NH * nz)
    three = 3 * ff
    keep = three - cross
    far = nz // 2
    pairs = nz // 2
    mirror = ns - 1 - sec

    def at_z(distance):
        return (z + distance + nz) % nz

    def device(s, h, zz):
        return (s, h * nz + zz)

    loads = []
    for b in (1, 0):
        for n, (src, dst) in enumerate(
            ((x_hbm, xb), (wg_hbm, wgb), (wu_hbm, wub), (y_hbm, yb), (wd_hbm, wdb))
        ):
            copy = pltpu.make_async_copy(src.at[0, b], dst.at[b], in_sem.at[b, n])
            copy.start()
            loads.append(copy)

    def load(b, n, src, dst):
        return pltpu.make_async_copy(src.at[0, b], dst.at[b], in_sem.at[b, n])

    barrier = pltpu.get_barrier_semaphore()
    neighbours = [
        device(sec, half, at_z(1)),
        device(sec, half, at_z(-1)),
        device(mirror, 0, z),
        device(mirror, 1, z),
        device(sec, 1 - half, z),
        device((sec + 1) % ns, half, z),
        device((sec + ns - 1) % ns, half, z),
    ]
    for target in neighbours:
        pl.semaphore_signal(barrier, inc=1, device_id=target, device_id_type=MESH)

    def forward(i, carry):
        b = 1 - i
        load(b, 0, x_hbm, xb).wait()
        load(b, 1, wg_hbm, wgb).wait()
        pre[0] = jnp.dot(xb[b], wgb[b], preferred_element_type=F32)
        load(b, 2, wu_hbm, wub).wait()
        pre[1] = jnp.dot(xb[b], wub[b], preferred_element_type=F32)
        load(b, 3, y_hbm, yb).wait()
        load(b, 4, wd_hbm, wdb).wait()
        pre[2] = lax.dot_general(
            yb[b], wdb[b], (((1,), (1,)), ((), ())), preferred_element_type=F32
        )
        step = min(128, tok)
        for row in range(0, tok, step):
            rows = pl.ds(row, step)
            gpre, upre, dhid = pre[0, rows, :], pre[1, rows, :], pre[2, rows, :]
            sig = jax.nn.sigmoid(gpre)
            activated = gpre * sig
            dgate = dhid * upre * sig * (1.0 + gpre * (1.0 - sig))
            dup = dhid * activated
            hidden = activated * upre
            act[b, 0, rows, :] = dgate.astype(BF16)
            act[b, 1, rows, :] = dup.astype(BF16)
            act_t[b, 0:ff, rows] = dgate.T.astype(BF16)
            act_t[b, ff : 2 * ff, rows] = dup.T.astype(BF16)
            act_t[b, 2 * ff : three, rows] = hidden.T.astype(BF16)
        return carry

    def weight_grad(b, h, pair):
        start = pl.multiple_of((h * nz + 2 * pair) * width, 2 * width)
        cols = pl.ds(start, 2 * width)
        gate_up = jnp.dot(act_t[b, 0 : 2 * ff, :], xb[b, :, cols], preferred_element_type=F32)
        part[b, h, 2 * pair, 0 : 2 * ff, :] = gate_up[:, :width].astype(BF16)
        part[b, h, 2 * pair + 1, 0 : 2 * ff, :] = gate_up[:, width:].astype(BF16)
        down = jnp.dot(act_t[b, 2 * ff : three, :], yb[b, :, cols], preferred_element_type=F32)
        for n in range(2):
            tile = down[:, n * width : (n + 1) * width].astype(BF16)
            if keep > 2 * ff:
                part[b, h, 2 * pair + n, 2 * ff : keep, :] = tile[: keep - 2 * ff]
            wide[b, h, 2 * pair + n] = tile[keep - 2 * ff :]

    def pair_at(piece):
        if pairs == 4:
            piece = (0, 3 - 2 * (z % 2), 1 + 2 * (z % 2), 2)[piece]
        return (z // 2 + far // 2 + piece) % pairs

    def wide_copy(n, piece):
        cols = pl.ds(2 * pair_at(piece), 2)
        if n < NH:
            src, target, slot = wide.at[1, n, cols], device(mirror, n, z), half
        else:
            src, target, slot = wide.at[0, 1 - half, cols], device(sec, 1 - half, z), NH
        return pltpu.make_async_remote_copy(
            src_ref=src,
            dst_ref=wide_in.at[slot, cols],
            send_sem=wide_send.at[n, piece],
            recv_sem=wide_recv.at[slot, piece],
            device_id=target,
            device_id_type=MESH,
        )

    def wide_wait(slot, piece):
        cols = pl.ds(2 * pair_at(piece), 2)
        pltpu.make_async_remote_copy(
            src_ref=wide.at[1, 0, cols],
            dst_ref=wide_in.at[slot, cols],
            send_sem=wide_send.at[0, piece],
            recv_sem=wide_recv.at[slot, piece],
            device_id=device(mirror, 0, z),
            device_id_type=MESH,
        ).wait_recv()

    part_rows = cross // 2

    def wide_message(direction, g, d):
        sign = -1 if direction == 0 else 1
        return pltpu.make_async_remote_copy(
            src_ref=wide.at[0, half, at_z(sign * d), pl.ds(g * part_rows, part_rows)],
            dst_ref=wide_ring.at[direction, g, d - 1],
            send_sem=wide_ring_send.at[direction, g, d - 1],
            recv_sem=wide_ring_recv.at[direction, g, d - 1],
            device_id=device(sec, half, at_z(sign)),
            device_id_type=MESH,
        )

    def wide_sum(target):
        total = wide[0, half, target].astype(F32)
        for slot in range(NH + 1):
            total = total + wide_in[slot, target].astype(F32)
        wide[0, half, target] = total.astype(BF16)

    def wide_accumulate(direction, g, d):
        sign = -1 if direction == 0 else 1
        wide_message(direction, g, d + 1).wait_recv()
        target = at_z(sign * d)
        rows = pl.ds(g * part_rows, part_rows)
        mine = wide[0, half, target, rows, :].astype(F32)
        wide[0, half, target, rows, :] = (mine + wide_ring[direction, g, d].astype(F32)).astype(BF16)

    def message(direction, h, d, b):
        sign = -1 if direction == 0 else 1
        return pltpu.make_async_remote_copy(
            src_ref=part.at[b, h, at_z(sign * d)],
            dst_ref=ring.at[direction, h, d - 1, b],
            send_sem=ring_send.at[direction, h, d - 1, b],
            recv_sem=ring_recv.at[direction, h, d - 1, b],
            device_id=device(sec, half, at_z(sign)),
            device_id_type=MESH,
        )

    def accumulate(direction, h, d, b):
        sign = -1 if direction == 0 else 1
        message(direction, h, d + 1, b).wait_recv()
        target = at_z(sign * d)
        mine = part[b, h, target].astype(F32)
        part[b, h, target] = (mine + ring[direction, h, d, b].astype(F32)).astype(BF16)

    long = ((0, 0), (1, 1))
    short = ((0, 1), (1, 0))

    def dx_copy(b):
        step = -1 if b == 0 else 1
        return pltpu.make_async_remote_copy(
            src_ref=dxb.at[b],
            dst_ref=gin.at[0, b],
            send_sem=dx_send.at[b],
            recv_sem=dx_recv.at[b],
            device_id=device(sec + step, half, z),
            device_id_type=MESH,
        )

    def zero_copy(b):
        return pltpu.make_async_copy(dxb.at[b], gin.at[0, 1 - b], zero_sem)

    cut = 2 * width

    def input_grad(b):
        def dx_chunk(j, carry):
            cols = pl.ds(pl.multiple_of(j * cut, cut), cut)
            contract = (((1,), (1,)), ((), ()))
            dx = lax.dot_general(
                act[b, 0], wgb[b, cols, :], contract, preferred_element_type=F32
            ) + lax.dot_general(act[b, 1], wub[b, cols, :], contract, preferred_element_type=F32)
            dxb[b, :, cols] = dx.astype(BF16)
            return carry

        sends = sec > 0 if b == 0 else sec < ns - 1

        @pl.when(sends)
        def _():
            lax.fori_loop(0, dim // cut, dx_chunk, 0)
            dx_copy(b).start()

        @pl.when(jnp.logical_not(sends))
        def _():
            dxb[b] = jnp.zeros((tok, dim), BF16)
            zero_copy(b).start()

    def ring_step(lanes, d, b):
        for direction, h in lanes:
            accumulate(direction, h, d, b)
            message(direction, h, d, b).start()

    def long_step(d, b):
        ring_step(long, d, b)

    def short_step(d, b):
        if d > 0:
            ring_step(short, d, b)

    def block(b, between):
        forward(1 - b, 0)
        for piece in range(pairs):
            pair = pair_at(piece)
            for h in range(NH):
                weight_grad(b, h, pair)
            if piece == 0:
                if b == 1:
                    pl.semaphore_wait(barrier, len(neighbours))
                for direction, h in long:
                    message(direction, h, far, b).start()
            if piece == 1 and far > 1:
                for direction, h in short:
                    message(direction, h, far - 1, b).start()
            for n in (0, 1) if b == 1 else (NH,):
                wide_copy(n, piece).start()
            between(piece)

    def wide_first():
        for slot in range(NH + 1):
            wide_wait(slot, 0)
        wide_sum(at_z(far))
        for direction, g in long:
            wide_message(direction, g, far).start()

    def wide_second():
        for slot in range(NH + 1):
            wide_wait(slot, 1)
        for sign in (-1, 1):
            wide_sum(at_z(sign * (far - 1)))
        for direction, g in short:
            wide_message(direction, g, far - 1).start()

    def wide_others():
        for piece in range(2, pairs):
            for slot in range(NH + 1):
                wide_wait(slot, piece)
        for d in range(far - 2, -1, -1):
            for sign in (-1, 1) if d > 0 else (1,):
                wide_sum(at_z(sign * d))

    def wide_step(lanes, d):
        for direction, g in lanes:
            wide_accumulate(direction, g, d)
            wide_message(direction, g, d).start()

    if far == 4:
        block(1, lambda piece: None)
        block(0, lambda piece: long_step(3, 1) if piece == 0 else None)
        short_step(2, 1)
        wide_first()
        long_step(3, 0)
        input_grad(1)
        wide_second()
        long_step(2, 1)
        input_grad(0)
        short_step(2, 0)
        short_step(1, 1)
        wide_others()
        long_step(2, 0)
        wide_step(long, 3)
        wide_step(short, 2)
        long_step(1, 1)
        short_step(1, 0)
        long_step(1, 0)
        wide_step(long, 2)
        wide_step(short, 1)
    else:
        block(1, lambda piece: None)
        block(0, lambda piece: None)
        input_grad(1)
        input_grad(0)
        wide_first()
        wide_second()
        wide_others()
        for d in range(far - 1, 0, -1):
            for b in (1, 0):
                long_step(d, b)
                short_step(d - 1, b)
            if d > 1:
                wide_step(long, d)
                if d > 2:
                    wide_step(short, d - 1)

    def reduced(b, h):
        return (
            part[b, h, z].astype(F32)
            + ring[0, h, 0, b].astype(F32)
            + ring[1, h, 0, b].astype(F32)
        )

    def finish_wait(b, h):
        message(0, h, 1, b).wait_recv()
        message(1, h, 1, b).wait_recv()

    def late_copy(n):
        if n < NH:
            target, slot = device(mirror, n, z), half
        else:
            target, slot = device(sec, 1 - half, z), NH
        return pltpu.make_async_remote_copy(
            src_ref=out1.at[n],
            dst_ref=late.at[slot],
            send_sem=late_send.at[n],
            recv_sem=late_recv.at[slot],
            device_id=target,
            device_id_type=MESH,
        )

    for h in range(NH):
        finish_wait(1, h)
        out1[h] = reduced(1, h).astype(BF16)
        late_copy(h).start()
    for h in range(NH):
        finish_wait(0, h)
    out1[NH] = reduced(0, 1 - half).astype(BF16)
    late_copy(NH).start()

    wide_step(long, 1)

    def late_wait(slot):
        pltpu.make_async_remote_copy(
            src_ref=out1.at[0],
            dst_ref=late.at[slot],
            send_sem=late_send.at[0],
            recv_sem=late_recv.at[slot],
            device_id=device(mirror, 0, z),
            device_id_type=MESH,
        ).wait_recv()

    for slot in range(3):
        late_wait(slot)
    for direction in range(2):
        for g in range(2):
            wide_message(direction, g, 1).wait_recv()

    def total_of(lo, hi):
        rows = pl.ds(lo, hi - lo)
        total = (
            part[0, half, z, rows, :].astype(F32)
            + ring[0, half, 0, 0, rows, :].astype(F32)
            + ring[1, half, 0, 0, rows, :].astype(F32)
        )
        for slot in range(3):
            total = total + late[slot, rows, :].astype(F32)
        return total

    pieces = [total_of(2 * ff, keep)] if keep > 2 * ff else []
    for g in range(2):
        rows = pl.ds(g * part_rows, part_rows)
        pieces.append(
            wide[0, half, z, rows, :].astype(F32)
            + wide_ring[0, g, 0].astype(F32)
            + wide_ring[1, g, 0].astype(F32)
        )
    total_ref[0:ff, :] = total_of(0, ff)
    total_ref[ff : 2 * ff, :] = total_of(ff, 2 * ff)
    total_ref[2 * ff : three, :] = jnp.concatenate(pieces, axis=0)

    for h in range(NH):
        late_copy(h).wait_send()
    late_copy(NH).wait_send()
    for n in range(NH + 1):
        for piece in range(pairs):
            wide_copy(n, piece).wait_send()
    for d in range(1, far + 1):
        for direction, g in long + (short if d < far else ()):
            wide_message(direction, g, d).wait_send()
    for b in range(2):
        for d in range(1, far + 1):
            for direction, h in long + (short if d < far else ()):
                message(direction, h, d, b).wait_send()

    @pl.when(sec > 0)
    def _():
        dx_copy(0).wait_send()
        dx_copy(1).wait_recv()

    @pl.when(sec < ns - 1)
    def _():
        dx_copy(1).wait_send()
        dx_copy(0).wait_recv()

    @pl.when(sec == 0)
    def _():
        zero_copy(0).wait()

    @pl.when(sec == ns - 1)
    def _():
        zero_copy(1).wait()


def finish_kernel(
    scale, gin, total_hbm, mg, mu, md, grad_in, ng, nu, nd,
    buf, total, mom, new, in_sem, out_sem, total_sem, mom_sem, new_sem,
):
    count, rows, _ = buf.shape
    per = gin.shape[2] // rows
    ff = total.shape[0] // 3

    def move(n, out):
        b, row = n // per, n % per * rows
        if out:
            return pltpu.make_async_copy(
                buf.at[n], grad_in.at[0, b, pl.ds(row, rows)], out_sem.at[n]
            )
        return pltpu.make_async_copy(gin.at[0, b, pl.ds(row, rows)], buf.at[n], in_sem.at[n])

    moms = [pltpu.make_async_copy(m.at[0], mom.at[n], mom_sem.at[n]) for n, m in enumerate((mg, mu, md))]
    news = [pltpu.make_async_copy(new.at[n], m.at[0], new_sem.at[n]) for n, m in enumerate((ng, nu, nd))]
    totals = pltpu.make_async_copy(total_hbm, total, total_sem)
    totals.start()
    for copy in moms:
        copy.start()
    for n in range(count):
        move(n, False).start()
    totals.wait()
    for n in range(3):
        moms[n].wait()
        new[n] = 0.9 * mom[n] + total[n * ff : (n + 1) * ff, :].T * scale
        news[n].start()
    for n in range(count):
        move(n, False).wait()
        move(n, True).start()
    for copy in news:
        copy.wait()
    for n in range(count):
        move(n, True).wait()


def body(inputs, cotangent, w_gate, w_up, w_down, mom_gate, mom_up, mom_down):
    ns = lax.axis_size("section")
    nz = lax.axis_size("dp") // NH
    _, _, tok, dim = inputs.shape
    ff = w_gate.shape[-1]
    far = nz // 2
    width = dim // (NH * nz)
    cross = int(3 * ff * CROSS) // 32 * 32
    keep = 3 * ff - cross
    anywhere = pl.BlockSpec(memory_space=pl.ANY)
    vmem = pl.BlockSpec(memory_space=pltpu.VMEM)
    dma = pltpu.SemaphoreType.DMA
    gin, total = pl.pallas_call(
        functools.partial(kernel, ns, nz, tok, dim, ff, cross),
        out_shape=(
            jax.ShapeDtypeStruct(inputs.shape, BF16),
            jax.ShapeDtypeStruct((3 * ff, width), F32),
        ),
        in_specs=[anywhere] * 5,
        out_specs=(anywhere, vmem),
        scratch_shapes=[
            pltpu.VMEM((2, tok, dim), BF16),
            pltpu.VMEM((2, tok, dim), BF16),
            pltpu.VMEM((2, dim, ff), BF16),
            pltpu.VMEM((2, dim, ff), BF16),
            pltpu.VMEM((2, ff, dim), BF16),
            pltpu.VMEM((2, 2, tok, ff), BF16),
            pltpu.VMEM((2, 3 * ff, tok), BF16),
            pltpu.VMEM((3, tok, ff), F32),
            pltpu.VMEM((2, NH, nz, keep, width), BF16),
            pltpu.VMEM((2, NH, far, 2, keep, width), BF16),
            pltpu.VMEM((2, tok, dim), BF16),
            pltpu.VMEM((NH + 1, keep, width), BF16),
            pltpu.VMEM((NH + 1, keep, width), BF16),
            pltpu.VMEM((2, NH, nz, cross, width), BF16),
            pltpu.VMEM((NH + 1, nz, cross, width), BF16),
            pltpu.VMEM((2, 2, far, cross // 2, width), BF16),
            dma((2, 5)),
            dma((2, NH, far, 2)),
            dma((2, NH, far, 2)),
            dma((2,)),
            dma((2,)),
            dma,
            dma((NH + 1,)),
            dma((NH + 1,)),
            dma((NH + 1, nz // 2)),
            dma((NH + 1, nz // 2)),
            dma((2, 2, far)),
            dma((2, 2, far)),
        ],
        compiler_params=pltpu.CompilerParams(
            collective_id=0, has_side_effects=True, vmem_limit_bytes=56 * 2**20
        ),
        name="relay_step",
    )(inputs, cotangent, w_gate, w_up, w_down)
    count = 4
    return pl.pallas_call(
        functools.partial(finish_kernel, 1.0 / float(tok * NH * nz) ** 0.5),
        out_shape=(
            jax.ShapeDtypeStruct(inputs.shape, BF16),
            jax.ShapeDtypeStruct(mom_gate.shape, F32),
            jax.ShapeDtypeStruct(mom_up.shape, F32),
            jax.ShapeDtypeStruct(mom_down.shape, F32),
        ),
        in_specs=[anywhere] * 5,
        out_specs=(anywhere,) * 4,
        scratch_shapes=[
            pltpu.VMEM((count, 2 * tok // count, dim), BF16),
            pltpu.VMEM((3 * ff, width), F32),
            pltpu.VMEM((3, width, ff), F32),
            pltpu.VMEM((3, width, ff), F32),
            dma((count,)),
            dma((count,)),
            dma,
            dma((3,)),
            dma((3,)),
        ],
        compiler_params=pltpu.CompilerParams(vmem_limit_bytes=56 * 2**20),
        name="relay_finish",
    )(gin, total, mom_gate, mom_up, mom_down)


def solution(mesh):
    placed = (
        P("section", None, "dp", None),
        P("section", None, "dp", None),
        P("section", None, None, None),
        P("section", None, None, None),
        P("section", None, None, None),
        P("section", "dp", None),
        P("section", "dp", None),
        P("section", "dp", None),
    )
    return jax.shard_map(
        body,
        mesh=mesh,
        in_specs=placed,
        out_specs=(
            P("section", None, "dp", None),
            P("section", "dp", None),
            P("section", "dp", None),
            P("section", "dp", None),
        ),
        check_vma=False,
    )
```

```python
import functools

import jax
import jax.numpy as jnp
from jax import lax
from jax.experimental import pallas as pl
from jax.experimental.pallas import tpu as pltpu
from jax.sharding import PartitionSpec as P

MESH = pl.DeviceIdType.MESH
NH = 2
CROSS = 0.2917
BF16 = jnp.bfloat16
F32 = jnp.float32


def kernel(
    ns, nz, tok, dim, ff, cross,
    x_hbm, y_hbm, wg_hbm, wu_hbm, wd_hbm,
    gin, total_ref,
    xb, yb, wgb, wub, wdb, act, act_t, pre, part, ring, dxb, out1, late,
    wide, wide_in, wide_ring,
    in_sem, ring_send, ring_recv, dx_send, dx_recv, zero_sem, late_send, late_recv,
    wide_send, wide_recv, wide_ring_send, wide_ring_recv,
):
    sec = lax.axis_index("section")
    dp = lax.axis_index("dp")
    half = dp // nz
    z = dp % nz
    width = dim // (NH * nz)
    three = 3 * ff
    keep = three - cross
    far = nz // 2
    pairs = nz // 2
    mirror = ns - 1 - sec

    def at_z(distance):
        return (z + distance + nz) % nz

    def device(s, h, zz):
        return (s, h * nz + zz)

    loads = []
    for b in (1, 0):
        for n, (src, dst) in enumerate(
            ((x_hbm, xb), (wg_hbm, wgb), (wu_hbm, wub), (y_hbm, yb), (wd_hbm, wdb))
        ):
            copy = pltpu.make_async_copy(src.at[0, b], dst.at[b], in_sem.at[b, n])
            copy.start()
            loads.append(copy)

    def load(b, n, src, dst):
        return pltpu.make_async_copy(src.at[0, b], dst.at[b], in_sem.at[b, n])

    barrier = pltpu.get_barrier_semaphore()
    neighbours = [
        device(sec, half, at_z(1)),
        device(sec, half, at_z(-1)),
        device(mirror, 0, z),
        device(mirror, 1, z),
        device(sec, 1 - half, z),
        device((sec + 1) % ns, half, z),
        device((sec + ns - 1) % ns, half, z),
    ]
    for target in neighbours:
        pl.semaphore_signal(barrier, inc=1, device_id=target, device_id_type=MESH)

    def forward(i, carry):
        b = 1 - i
        load(b, 0, x_hbm, xb).wait()
        load(b, 1, wg_hbm, wgb).wait()
        pre[0] = jnp.dot(xb[b], wgb[b], preferred_element_type=F32)
        load(b, 2, wu_hbm, wub).wait()
        pre[1] = jnp.dot(xb[b], wub[b], preferred_element_type=F32)
        load(b, 3, y_hbm, yb).wait()
        load(b, 4, wd_hbm, wdb).wait()
        pre[2] = lax.dot_general(
            yb[b], wdb[b], (((1,), (1,)), ((), ())), preferred_element_type=F32
        )
        step = min(128, tok)
        for row in range(0, tok, step):
            rows = pl.ds(row, step)
            gpre, upre, dhid = pre[0, rows, :], pre[1, rows, :], pre[2, rows, :]
            sig = jax.nn.sigmoid(gpre)
            activated = gpre * sig
            dgate = dhid * upre * sig * (1.0 + gpre * (1.0 - sig))
            dup = dhid * activated
            hidden = activated * upre
            act[b, 0, rows, :] = dgate.astype(BF16)
            act[b, 1, rows, :] = dup.astype(BF16)
            act_t[b, 0:ff, rows] = dgate.T.astype(BF16)
            act_t[b, ff : 2 * ff, rows] = dup.T.astype(BF16)
            act_t[b, 2 * ff : three, rows] = hidden.T.astype(BF16)
        return carry

    def weight_grad(b, h, pair):
        start = pl.multiple_of((h * nz + 2 * pair) * width, 2 * width)
        cols = pl.ds(start, 2 * width)
        gate_up = jnp.dot(act_t[b, 0 : 2 * ff, :], xb[b, :, cols], preferred_element_type=F32)
        part[b, h, 2 * pair, 0 : 2 * ff, :] = gate_up[:, :width].astype(BF16)
        part[b, h, 2 * pair + 1, 0 : 2 * ff, :] = gate_up[:, width:].astype(BF16)
        down = jnp.dot(act_t[b, 2 * ff : three, :], yb[b, :, cols], preferred_element_type=F32)
        for n in range(2):
            tile = down[:, n * width : (n + 1) * width].astype(BF16)
            if keep > 2 * ff:
                part[b, h, 2 * pair + n, 2 * ff : keep, :] = tile[: keep - 2 * ff]
            wide[b, h, 2 * pair + n] = tile[keep - 2 * ff :]

    def pair_at(piece):
        if pairs == 4:
            piece = (0, 3 - 2 * (z % 2), 1 + 2 * (z % 2), 2)[piece]
        return (z // 2 + far // 2 + piece) % pairs

    def wide_copy(n, piece):
        cols = pl.ds(2 * pair_at(piece), 2)
        if n < NH:
            src, target, slot = wide.at[1, n, cols], device(mirror, n, z), half
        else:
            src, target, slot = wide.at[0, 1 - half, cols], device(sec, 1 - half, z), NH
        return pltpu.make_async_remote_copy(
            src_ref=src,
            dst_ref=wide_in.at[slot, cols],
            send_sem=wide_send.at[n, piece],
            recv_sem=wide_recv.at[slot, piece],
            device_id=target,
            device_id_type=MESH,
        )

    def wide_wait(slot, piece):
        cols = pl.ds(2 * pair_at(piece), 2)
        pltpu.make_async_remote_copy(
            src_ref=wide.at[1, 0, cols],
            dst_ref=wide_in.at[slot, cols],
            send_sem=wide_send.at[0, piece],
            recv_sem=wide_recv.at[slot, piece],
            device_id=device(mirror, 0, z),
            device_id_type=MESH,
        ).wait_recv()

    part_rows = cross // 2

    def wide_message(direction, g, d):
        sign = -1 if direction == 0 else 1
        return pltpu.make_async_remote_copy(
            src_ref=wide.at[0, half, at_z(sign * d), pl.ds(g * part_rows, part_rows)],
            dst_ref=wide_ring.at[direction, g, d - 1],
            send_sem=wide_ring_send.at[direction, g, d - 1],
            recv_sem=wide_ring_recv.at[direction, g, d - 1],
            device_id=device(sec, half, at_z(sign)),
            device_id_type=MESH,
        )

    def wide_sum(target):
        total = wide[0, half, target].astype(F32)
        for slot in range(NH + 1):
            total = total + wide_in[slot, target].astype(F32)
        wide[0, half, target] = total.astype(BF16)

    def wide_accumulate(direction, g, d):
        sign = -1 if direction == 0 else 1
        wide_message(direction, g, d + 1).wait_recv()
        target = at_z(sign * d)
        rows = pl.ds(g * part_rows, part_rows)
        mine = wide[0, half, target, rows, :].astype(F32)
        wide[0, half, target, rows, :] = (mine + wide_ring[direction, g, d].astype(F32)).astype(BF16)

    def message(direction, h, d, b):
        sign = -1 if direction == 0 else 1
        return pltpu.make_async_remote_copy(
            src_ref=part.at[b, h, at_z(sign * d)],
            dst_ref=ring.at[direction, h, d - 1, b],
            send_sem=ring_send.at[direction, h, d - 1, b],
            recv_sem=ring_recv.at[direction, h, d - 1, b],
            device_id=device(sec, half, at_z(sign)),
            device_id_type=MESH,
        )

    def accumulate(direction, h, d, b):
        sign = -1 if direction == 0 else 1
        message(direction, h, d + 1, b).wait_recv()
        target = at_z(sign * d)
        mine = part[b, h, target].astype(F32)
        part[b, h, target] = (mine + ring[direction, h, d, b].astype(F32)).astype(BF16)

    long = ((0, 0), (1, 1))
    short = ((0, 1), (1, 0))

    def dx_copy(b):
        step = -1 if b == 0 else 1
        return pltpu.make_async_remote_copy(
            src_ref=dxb.at[b],
            dst_ref=gin.at[0, b],
            send_sem=dx_send.at[b],
            recv_sem=dx_recv.at[b],
            device_id=device(sec + step, half, z),
            device_id_type=MESH,
        )

    def zero_copy(b):
        return pltpu.make_async_copy(dxb.at[b], gin.at[0, 1 - b], zero_sem)

    cut = 2 * width

    def input_grad(b):
        def dx_chunk(j, carry):
            cols = pl.ds(pl.multiple_of(j * cut, cut), cut)
            contract = (((1,), (1,)), ((), ()))
            dx = lax.dot_general(
                act[b, 0], wgb[b, cols, :], contract, preferred_element_type=F32
            ) + lax.dot_general(act[b, 1], wub[b, cols, :], contract, preferred_element_type=F32)
            dxb[b, :, cols] = dx.astype(BF16)
            return carry

        sends = sec > 0 if b == 0 else sec < ns - 1

        @pl.when(sends)
        def _():
            lax.fori_loop(0, dim // cut, dx_chunk, 0)

        @pl.when(jnp.logical_not(sends))
        def _():
            dxb[b] = jnp.zeros((tok, dim), BF16)
            zero_copy(b).start()

    def send_dx(b):
        @pl.when(sec > 0 if b == 0 else sec < ns - 1)
        def _():
            dx_copy(b).start()

    def ring_step(lanes, d, b):
        for direction, h in lanes:
            accumulate(direction, h, d, b)
            message(direction, h, d, b).start()

    def long_step(d, b):
        ring_step(long, d, b)

    def short_step(d, b):
        if d > 0:
            ring_step(short, d, b)

    def block(b, between):
        forward(1 - b, 0)
        for piece in range(pairs):
            pair = pair_at(piece)
            for h in range(NH):
                weight_grad(b, h, pair)
            if piece == 0:
                if b == 1:
                    pl.semaphore_wait(barrier, len(neighbours))
                for direction, h in long:
                    message(direction, h, far, b).start()
            if piece == 1 and far > 1:
                for direction, h in short:
                    message(direction, h, far - 1, b).start()
            for n in (0, 1) if b == 1 else (NH,):
                wide_copy(n, piece).start()
            between(piece)

    def wide_first():
        for slot in range(NH + 1):
            wide_wait(slot, 0)
        wide_sum(at_z(far))
        for direction, g in long:
            wide_message(direction, g, far).start()

    def wide_second():
        for slot in range(NH + 1):
            wide_wait(slot, 1)
        for sign in (-1, 1):
            wide_sum(at_z(sign * (far - 1)))
        for direction, g in short:
            wide_message(direction, g, far - 1).start()

    def wide_others():
        for piece in range(2, pairs):
            for slot in range(NH + 1):
                wide_wait(slot, piece)
        for d in range(far - 2, -1, -1):
            for sign in (-1, 1) if d > 0 else (1,):
                wide_sum(at_z(sign * d))

    def wide_step(lanes, d):
        for direction, g in lanes:
            wide_accumulate(direction, g, d)
            wide_message(direction, g, d).start()

    if far == 4:
        block(1, lambda piece: None)
        block(0, lambda piece: long_step(3, 1) if piece == 0 else None)
        short_step(2, 1)
        wide_first()
        long_step(3, 0)
        input_grad(1)
        wide_second()
        long_step(2, 1)
        input_grad(0)
        short_step(2, 0)
        short_step(1, 1)

        wide_others()
        send_dx(1)
        send_dx(0)
        long_step(2, 0)
        wide_step(long, 3)
        wide_step(short, 2)
        long_step(1, 1)
        short_step(1, 0)
        long_step(1, 0)
        wide_step(long, 2)
        wide_step(short, 1)
    else:
        block(1, lambda piece: None)
        block(0, lambda piece: None)
        input_grad(1)
        input_grad(0)
        send_dx(1)
        send_dx(0)
        wide_first()
        wide_second()
        wide_others()
        for d in range(far - 1, 0, -1):
            for b in (1, 0):
                long_step(d, b)
                short_step(d - 1, b)
            if d > 1:
                wide_step(long, d)
                if d > 2:
                    wide_step(short, d - 1)

    def reduced(b, h):
        return (
            part[b, h, z].astype(F32)
            + ring[0, h, 0, b].astype(F32)
            + ring[1, h, 0, b].astype(F32)
        )

    def finish_wait(b, h):
        message(0, h, 1, b).wait_recv()
        message(1, h, 1, b).wait_recv()

    def late_copy(n):
        if n < NH:
            target, slot = device(mirror, n, z), half
        else:
            target, slot = device(sec, 1 - half, z), NH
        return pltpu.make_async_remote_copy(
            src_ref=out1.at[n],
            dst_ref=late.at[slot],
            send_sem=late_send.at[n],
            recv_sem=late_recv.at[slot],
            device_id=target,
            device_id_type=MESH,
        )

    for h in range(NH):
        finish_wait(1, h)
        out1[h] = reduced(1, h).astype(BF16)
        late_copy(h).start()
    for h in range(NH):
        finish_wait(0, h)
    out1[NH] = reduced(0, 1 - half).astype(BF16)
    late_copy(NH).start()

    wide_step(long, 1)

    def late_wait(slot):
        pltpu.make_async_remote_copy(
            src_ref=out1.at[0],
            dst_ref=late.at[slot],
            send_sem=late_send.at[0],
            recv_sem=late_recv.at[slot],
            device_id=device(mirror, 0, z),
            device_id_type=MESH,
        ).wait_recv()

    for slot in range(3):
        late_wait(slot)
    for direction in range(2):
        for g in range(2):
            wide_message(direction, g, 1).wait_recv()

    def total_of(lo, hi):
        rows = pl.ds(lo, hi - lo)
        total = (
            part[0, half, z, rows, :].astype(F32)
            + ring[0, half, 0, 0, rows, :].astype(F32)
            + ring[1, half, 0, 0, rows, :].astype(F32)
        )
        for slot in range(3):
            total = total + late[slot, rows, :].astype(F32)
        return total

    pieces = [total_of(2 * ff, keep)] if keep > 2 * ff else []
    for g in range(2):
        rows = pl.ds(g * part_rows, part_rows)
        pieces.append(
            wide[0, half, z, rows, :].astype(F32)
            + wide_ring[0, g, 0].astype(F32)
            + wide_ring[1, g, 0].astype(F32)
        )
    total_ref[0:ff, :] = total_of(0, ff)
    total_ref[ff : 2 * ff, :] = total_of(ff, 2 * ff)
    total_ref[2 * ff : three, :] = jnp.concatenate(pieces, axis=0)

    for h in range(NH):
        late_copy(h).wait_send()
    late_copy(NH).wait_send()
    for n in range(NH + 1):
        for piece in range(pairs):
            wide_copy(n, piece).wait_send()
    for d in range(1, far + 1):
        for direction, g in long + (short if d < far else ()):
            wide_message(direction, g, d).wait_send()
    for b in range(2):
        for d in range(1, far + 1):
            for direction, h in long + (short if d < far else ()):
                message(direction, h, d, b).wait_send()

    @pl.when(sec > 0)
    def _():
        dx_copy(0).wait_send()
        dx_copy(1).wait_recv()

    @pl.when(sec < ns - 1)
    def _():
        dx_copy(1).wait_send()
        dx_copy(0).wait_recv()

    @pl.when(sec == 0)
    def _():
        zero_copy(0).wait()

    @pl.when(sec == ns - 1)
    def _():
        zero_copy(1).wait()


def finish_kernel(
    scale, gin, total_hbm, mg, mu, md, grad_in, ng, nu, nd,
    buf, total, mom, new, in_sem, out_sem, total_sem, mom_sem, new_sem,
):
    count, rows, _ = buf.shape
    per = gin.shape[2] // rows
    ff = total.shape[0] // 3

    def move(n, out):
        b, row = n // per, n % per * rows
        if out:
            return pltpu.make_async_copy(
                buf.at[n], grad_in.at[0, b, pl.ds(row, rows)], out_sem.at[n]
            )
        return pltpu.make_async_copy(gin.at[0, b, pl.ds(row, rows)], buf.at[n], in_sem.at[n])

    moms = [pltpu.make_async_copy(m.at[0], mom.at[n], mom_sem.at[n]) for n, m in enumerate((mg, mu, md))]
    news = [pltpu.make_async_copy(new.at[n], m.at[0], new_sem.at[n]) for n, m in enumerate((ng, nu, nd))]
    totals = pltpu.make_async_copy(total_hbm, total, total_sem)
    totals.start()
    for copy in moms:
        copy.start()
    for n in range(count):
        move(n, False).start()
    totals.wait()
    for n in range(3):
        moms[n].wait()
        new[n] = 0.9 * mom[n] + total[n * ff : (n + 1) * ff, :].T * scale
        news[n].start()
    for n in range(count):
        move(n, False).wait()
        move(n, True).start()
    for copy in news:
        copy.wait()
    for n in range(count):
        move(n, True).wait()


def body(inputs, cotangent, w_gate, w_up, w_down, mom_gate, mom_up, mom_down):
    ns = lax.axis_size("section")
    nz = lax.axis_size("dp") // NH
    _, _, tok, dim = inputs.shape
    ff = w_gate.shape[-1]
    far = nz // 2
    width = dim // (NH * nz)
    cross = int(3 * ff * CROSS) // 32 * 32
    keep = 3 * ff - cross
    anywhere = pl.BlockSpec(memory_space=pl.ANY)
    vmem = pl.BlockSpec(memory_space=pltpu.VMEM)
    dma = pltpu.SemaphoreType.DMA
    gin, total = pl.pallas_call(
        functools.partial(kernel, ns, nz, tok, dim, ff, cross),
        out_shape=(
            jax.ShapeDtypeStruct(inputs.shape, BF16),
            jax.ShapeDtypeStruct((3 * ff, width), F32),
        ),
        in_specs=[anywhere] * 5,
        out_specs=(anywhere, vmem),
        scratch_shapes=[
            pltpu.VMEM((2, tok, dim), BF16),
            pltpu.VMEM((2, tok, dim), BF16),
            pltpu.VMEM((2, dim, ff), BF16),
            pltpu.VMEM((2, dim, ff), BF16),
            pltpu.VMEM((2, ff, dim), BF16),
            pltpu.VMEM((2, 2, tok, ff), BF16),
            pltpu.VMEM((2, 3 * ff, tok), BF16),
            pltpu.VMEM((3, tok, ff), F32),
            pltpu.VMEM((2, NH, nz, keep, width), BF16),
            pltpu.VMEM((2, NH, far, 2, keep, width), BF16),
            pltpu.VMEM((2, tok, dim), BF16),
            pltpu.VMEM((NH + 1, keep, width), BF16),
            pltpu.VMEM((NH + 1, keep, width), BF16),
            pltpu.VMEM((2, NH, nz, cross, width), BF16),
            pltpu.VMEM((NH + 1, nz, cross, width), BF16),
            pltpu.VMEM((2, 2, far, cross // 2, width), BF16),
            dma((2, 5)),
            dma((2, NH, far, 2)),
            dma((2, NH, far, 2)),
            dma((2,)),
            dma((2,)),
            dma,
            dma((NH + 1,)),
            dma((NH + 1,)),
            dma((NH + 1, nz // 2)),
            dma((NH + 1, nz // 2)),
            dma((2, 2, far)),
            dma((2, 2, far)),
        ],
        compiler_params=pltpu.CompilerParams(
            collective_id=0, has_side_effects=True, vmem_limit_bytes=56 * 2**20
        ),
        name="relay_step",
    )(inputs, cotangent, w_gate, w_up, w_down)
    count = 4
    return pl.pallas_call(
        functools.partial(finish_kernel, 1.0 / float(tok * NH * nz) ** 0.5),
        out_shape=(
            jax.ShapeDtypeStruct(inputs.shape, BF16),
            jax.ShapeDtypeStruct(mom_gate.shape, F32),
            jax.ShapeDtypeStruct(mom_up.shape, F32),
            jax.ShapeDtypeStruct(mom_down.shape, F32),
        ),
        in_specs=[anywhere] * 5,
        out_specs=(anywhere,) * 4,
        scratch_shapes=[
            pltpu.VMEM((count, 2 * tok // count, dim), BF16),
            pltpu.VMEM((3 * ff, width), F32),
            pltpu.VMEM((3, width, ff), F32),
            pltpu.VMEM((3, width, ff), F32),
            dma((count,)),
            dma((count,)),
            dma,
            dma((3,)),
            dma((3,)),
        ],
        compiler_params=pltpu.CompilerParams(vmem_limit_bytes=56 * 2**20),
        name="relay_finish",
    )(gin, total, mom_gate, mom_up, mom_down)


def solution(mesh):
    placed = (
        P("section", None, "dp", None),
        P("section", None, "dp", None),
        P("section", None, None, None),
        P("section", None, None, None),
        P("section", None, None, None),
        P("section", "dp", None),
        P("section", "dp", None),
        P("section", "dp", None),
    )
    return jax.shard_map(
        body,
        mesh=mesh,
        in_specs=placed,
        out_specs=(
            P("section", None, "dp", None),
            P("section", "dp", None),
            P("section", "dp", None),
            P("section", "dp", None),
        ),
        check_vma=False,
    )
```

```python
import functools

import jax
import jax.numpy as jnp
from jax import lax
from jax.experimental import pallas as pl
from jax.experimental.pallas import tpu as pltpu
from jax.sharding import PartitionSpec as P

MESH = pl.DeviceIdType.MESH
NH = 2
CROSS = 0.2917
BF16 = jnp.bfloat16
F32 = jnp.float32


def kernel(
    ns, nz, tok, dim, ff, cross,
    x_hbm, y_hbm, wg_hbm, wu_hbm, wd_hbm,
    gin, total_ref,
    xb, yb, wgb, wub, wdb, act, act_t, pre, part, ring, dxb, out1, late,
    wide, wide_in, wide_ring,
    in_sem, ring_send, ring_recv, dx_send, dx_recv, zero_sem, late_send, late_recv,
    wide_send, wide_recv, wide_ring_send, wide_ring_recv,
):
    sec = lax.axis_index("section")
    dp = lax.axis_index("dp")
    half = dp // nz
    z = dp % nz
    width = dim // (NH * nz)
    three = 3 * ff
    keep = three - cross
    far = nz // 2
    pairs = nz // 2
    mirror = ns - 1 - sec

    def at_z(distance):
        return (z + distance + nz) % nz

    def device(s, h, zz):
        return (s, h * nz + zz)

    def start_loads(b):
        for n, (src, dst) in enumerate(
            ((x_hbm, xb), (wg_hbm, wgb), (wu_hbm, wub), (y_hbm, yb), (wd_hbm, wdb))
        ):
            load(b, n, src, dst).start()

    def load(b, n, src, dst):
        return pltpu.make_async_copy(src.at[0, b], dst.at[b], in_sem.at[b, n])

    start_loads(1)

    barrier = pltpu.get_barrier_semaphore()
    neighbours = [
        device(sec, half, at_z(1)),
        device(sec, half, at_z(-1)),
        device(mirror, 0, z),
        device(mirror, 1, z),
        device(sec, 1 - half, z),
        device((sec + 1) % ns, half, z),
        device((sec + ns - 1) % ns, half, z),
    ]
    for target in neighbours:
        pl.semaphore_signal(barrier, inc=1, device_id=target, device_id_type=MESH)

    def forward(i, carry):
        b = 1 - i
        load(b, 0, x_hbm, xb).wait()
        load(b, 1, wg_hbm, wgb).wait()
        if b == 1:
            start_loads(0)
        pre[0] = jnp.dot(xb[b], wgb[b], preferred_element_type=F32)
        load(b, 2, wu_hbm, wub).wait()
        pre[1] = jnp.dot(xb[b], wub[b], preferred_element_type=F32)
        load(b, 3, y_hbm, yb).wait()
        load(b, 4, wd_hbm, wdb).wait()
        pre[2] = lax.dot_general(
            yb[b], wdb[b], (((1,), (1,)), ((), ())), preferred_element_type=F32
        )
        step = min(128, tok)
        for row in range(0, tok, step):
            rows = pl.ds(row, step)
            gpre, upre, dhid = pre[0, rows, :], pre[1, rows, :], pre[2, rows, :]
            sig = jax.nn.sigmoid(gpre)
            activated = gpre * sig
            dgate = dhid * upre * sig * (1.0 + gpre * (1.0 - sig))
            dup = dhid * activated
            hidden = activated * upre
            act[b, 0, rows, :] = dgate.astype(BF16)
            act[b, 1, rows, :] = dup.astype(BF16)
            act_t[b, 0:ff, rows] = dgate.T.astype(BF16)
            act_t[b, ff : 2 * ff, rows] = dup.T.astype(BF16)
            act_t[b, 2 * ff : three, rows] = hidden.T.astype(BF16)
        return carry

    def weight_grad(b, h, pair):
        start = pl.multiple_of((h * nz + 2 * pair) * width, 2 * width)
        cols = pl.ds(start, 2 * width)
        gate_up = jnp.dot(act_t[b, 0 : 2 * ff, :], xb[b, :, cols], preferred_element_type=F32)
        part[b, h, 2 * pair, 0 : 2 * ff, :] = gate_up[:, :width].astype(BF16)
        part[b, h, 2 * pair + 1, 0 : 2 * ff, :] = gate_up[:, width:].astype(BF16)
        down = jnp.dot(act_t[b, 2 * ff : three, :], yb[b, :, cols], preferred_element_type=F32)
        for n in range(2):
            tile = down[:, n * width : (n + 1) * width].astype(BF16)
            if keep > 2 * ff:
                part[b, h, 2 * pair + n, 2 * ff : keep, :] = tile[: keep - 2 * ff]
            wide[b, h, 2 * pair + n] = tile[keep - 2 * ff :]

    def pair_at(piece):
        if pairs == 4:
            piece = (0, 3 - 2 * (z % 2), 1 + 2 * (z % 2), 2)[piece]
        return (z // 2 + far // 2 + piece) % pairs

    def wide_copy(n, piece):
        cols = pl.ds(2 * pair_at(piece), 2)
        if n < NH:
            src, target, slot = wide.at[1, n, cols], device(mirror, n, z), half
        else:
            src, target, slot = wide.at[0, 1 - half, cols], device(sec, 1 - half, z), NH
        return pltpu.make_async_remote_copy(
            src_ref=src,
            dst_ref=wide_in.at[slot, cols],
            send_sem=wide_send.at[n, piece],
            recv_sem=wide_recv.at[slot, piece],
            device_id=target,
            device_id_type=MESH,
        )

    def wide_wait(slot, piece):
        cols = pl.ds(2 * pair_at(piece), 2)
        pltpu.make_async_remote_copy(
            src_ref=wide.at[1, 0, cols],
            dst_ref=wide_in.at[slot, cols],
            send_sem=wide_send.at[0, piece],
            recv_sem=wide_recv.at[slot, piece],
            device_id=device(mirror, 0, z),
            device_id_type=MESH,
        ).wait_recv()

    part_rows = cross // 2

    def wide_message(direction, g, d):
        sign = -1 if direction == 0 else 1
        return pltpu.make_async_remote_copy(
            src_ref=wide.at[0, half, at_z(sign * d), pl.ds(g * part_rows, part_rows)],
            dst_ref=wide_ring.at[direction, g, d - 1],
            send_sem=wide_ring_send.at[direction, g, d - 1],
            recv_sem=wide_ring_recv.at[direction, g, d - 1],
            device_id=device(sec, half, at_z(sign)),
            device_id_type=MESH,
        )

    def wide_sum(target):
        total = wide[0, half, target].astype(F32)
        for slot in range(NH + 1):
            total = total + wide_in[slot, target].astype(F32)
        wide[0, half, target] = total.astype(BF16)

    def wide_accumulate(direction, g, d):
        sign = -1 if direction == 0 else 1
        wide_message(direction, g, d + 1).wait_recv()
        target = at_z(sign * d)
        rows = pl.ds(g * part_rows, part_rows)
        mine = wide[0, half, target, rows, :].astype(F32)
        wide[0, half, target, rows, :] = (mine + wide_ring[direction, g, d].astype(F32)).astype(BF16)

    def message(direction, h, d, b):
        sign = -1 if direction == 0 else 1
        return pltpu.make_async_remote_copy(
            src_ref=part.at[b, h, at_z(sign * d)],
            dst_ref=ring.at[direction, h, d - 1, b],
            send_sem=ring_send.at[direction, h, d - 1, b],
            recv_sem=ring_recv.at[direction, h, d - 1, b],
            device_id=device(sec, half, at_z(sign)),
            device_id_type=MESH,
        )

    def accumulate(direction, h, d, b):
        sign = -1 if direction == 0 else 1
        message(direction, h, d + 1, b).wait_recv()
        target = at_z(sign * d)
        mine = part[b, h, target].astype(F32)
        part[b, h, target] = (mine + ring[direction, h, d, b].astype(F32)).astype(BF16)

    long = ((0, 0), (1, 1))
    short = ((0, 1), (1, 0))

    def dx_copy(b):
        step = -1 if b == 0 else 1
        return pltpu.make_async_remote_copy(
            src_ref=dxb.at[b],
            dst_ref=gin.at[0, b],
            send_sem=dx_send.at[b],
            recv_sem=dx_recv.at[b],
            device_id=device(sec + step, half, z),
            device_id_type=MESH,
        )

    def zero_copy(b):
        return pltpu.make_async_copy(dxb.at[b], gin.at[0, 1 - b], zero_sem)

    cut = 2 * width

    def input_grad(b):
        def dx_chunk(j, carry):
            cols = pl.ds(pl.multiple_of(j * cut, cut), cut)
            contract = (((1,), (1,)), ((), ()))
            dx = lax.dot_general(
                act[b, 0], wgb[b, cols, :], contract, preferred_element_type=F32
            ) + lax.dot_general(act[b, 1], wub[b, cols, :], contract, preferred_element_type=F32)
            dxb[b, :, cols] = dx.astype(BF16)
            return carry

        sends = sec > 0 if b == 0 else sec < ns - 1

        @pl.when(sends)
        def _():
            lax.fori_loop(0, dim // cut, dx_chunk, 0)

        @pl.when(jnp.logical_not(sends))
        def _():
            dxb[b] = jnp.zeros((tok, dim), BF16)
            zero_copy(b).start()

    def send_dx(b):
        @pl.when(sec > 0 if b == 0 else sec < ns - 1)
        def _():
            dx_copy(b).start()

    def ring_step(lanes, d, b):
        for direction, h in lanes:
            accumulate(direction, h, d, b)
            message(direction, h, d, b).start()

    def long_step(d, b):
        ring_step(long, d, b)

    def short_step(d, b):
        if d > 0:
            ring_step(short, d, b)

    def block(b, between):
        forward(1 - b, 0)
        for piece in range(pairs):
            pair = pair_at(piece)
            for h in range(NH):
                weight_grad(b, h, pair)
            if piece == 0:
                if b == 1:
                    pl.semaphore_wait(barrier, len(neighbours))
                for direction, h in long:
                    message(direction, h, far, b).start()
            if piece == 1 and far > 1:
                for direction, h in short:
                    message(direction, h, far - 1, b).start()
            for n in (0, 1) if b == 1 else (NH,):
                wide_copy(n, piece).start()
            between(piece)

    def wide_first():
        for slot in range(NH + 1):
            wide_wait(slot, 0)
        wide_sum(at_z(far))
        for direction, g in long:
            wide_message(direction, g, far).start()

    def wide_second():
        for slot in range(NH + 1):
            wide_wait(slot, 1)
        for sign in (-1, 1):
            wide_sum(at_z(sign * (far - 1)))
        for direction, g in short:
            wide_message(direction, g, far - 1).start()

    def wide_others():
        for piece in range(2, pairs):
            for slot in range(NH + 1):
                wide_wait(slot, piece)
        for d in range(far - 2, -1, -1):
            for sign in (-1, 1) if d > 0 else (1,):
                wide_sum(at_z(sign * d))

    def wide_step(lanes, d):
        for direction, g in lanes:
            wide_accumulate(direction, g, d)
            wide_message(direction, g, d).start()

    if far == 4:
        block(1, lambda piece: None)
        block(0, lambda piece: long_step(3, 1) if piece == 0 else None)
        short_step(2, 1)
        wide_first()
        long_step(3, 0)
        input_grad(1)
        wide_second()
        long_step(2, 1)
        input_grad(0)
        short_step(2, 0)
        wide_others()
        send_dx(1)
        send_dx(0)
        short_step(1, 1)
        long_step(2, 0)
        wide_step(long, 3)
        wide_step(short, 2)
        long_step(1, 1)
        short_step(1, 0)
        wide_step(long, 2)
        wide_step(short, 1)
        long_step(1, 0)
    else:
        block(1, lambda piece: None)
        block(0, lambda piece: None)
        input_grad(1)
        input_grad(0)
        send_dx(1)
        send_dx(0)
        wide_first()
        wide_second()
        wide_others()
        for d in range(far - 1, 0, -1):
            for b in (1, 0):
                long_step(d, b)
                short_step(d - 1, b)
            if d > 1:
                wide_step(long, d)
                if d > 2:
                    wide_step(short, d - 1)

    def reduced(b, h):
        return (
            part[b, h, z].astype(F32)
            + ring[0, h, 0, b].astype(F32)
            + ring[1, h, 0, b].astype(F32)
        )

    def finish_wait(b, h):
        message(0, h, 1, b).wait_recv()
        message(1, h, 1, b).wait_recv()

    def late_copy(n):
        if n < NH:
            target, slot = device(mirror, n, z), half
        else:
            target, slot = device(sec, 1 - half, z), NH
        return pltpu.make_async_remote_copy(
            src_ref=out1.at[n],
            dst_ref=late.at[slot],
            send_sem=late_send.at[n],
            recv_sem=late_recv.at[slot],
            device_id=target,
            device_id_type=MESH,
        )

    for h in range(NH):
        finish_wait(1, h)
        out1[h] = reduced(1, h).astype(BF16)
        late_copy(h).start()
    for h in range(NH):
        finish_wait(0, h)
    out1[NH] = reduced(0, 1 - half).astype(BF16)
    late_copy(NH).start()

    wide_step(long, 1)

    def late_wait(slot):
        pltpu.make_async_remote_copy(
            src_ref=out1.at[0],
            dst_ref=late.at[slot],
            send_sem=late_send.at[0],
            recv_sem=late_recv.at[slot],
            device_id=device(mirror, 0, z),
            device_id_type=MESH,
        ).wait_recv()

    for slot in range(3):
        late_wait(slot)
    for direction in range(2):
        for g in range(2):
            wide_message(direction, g, 1).wait_recv()

    def total_of(lo, hi):
        rows = pl.ds(lo, hi - lo)
        total = (
            part[0, half, z, rows, :].astype(F32)
            + ring[0, half, 0, 0, rows, :].astype(F32)
            + ring[1, half, 0, 0, rows, :].astype(F32)
        )
        for slot in range(3):
            total = total + late[slot, rows, :].astype(F32)
        return total

    pieces = [total_of(2 * ff, keep)] if keep > 2 * ff else []
    for g in range(2):
        rows = pl.ds(g * part_rows, part_rows)
        pieces.append(
            wide[0, half, z, rows, :].astype(F32)
            + wide_ring[0, g, 0].astype(F32)
            + wide_ring[1, g, 0].astype(F32)
        )
    total_ref[0:ff, :] = total_of(0, ff)
    total_ref[ff : 2 * ff, :] = total_of(ff, 2 * ff)
    total_ref[2 * ff : three, :] = jnp.concatenate(pieces, axis=0)

    for h in range(NH):
        late_copy(h).wait_send()
    late_copy(NH).wait_send()
    for n in range(NH + 1):
        for piece in range(pairs):
            wide_copy(n, piece).wait_send()
    for d in range(1, far + 1):
        for direction, g in long + (short if d < far else ()):
            wide_message(direction, g, d).wait_send()
    for b in range(2):
        for d in range(1, far + 1):
            for direction, h in long + (short if d < far else ()):
                message(direction, h, d, b).wait_send()

    @pl.when(sec > 0)
    def _():
        dx_copy(0).wait_send()
        dx_copy(1).wait_recv()

    @pl.when(sec < ns - 1)
    def _():
        dx_copy(1).wait_send()
        dx_copy(0).wait_recv()

    @pl.when(sec == 0)
    def _():
        zero_copy(0).wait()

    @pl.when(sec == ns - 1)
    def _():
        zero_copy(1).wait()


def finish_kernel(
    scale, gin, total_hbm, mg, mu, md, grad_in, ng, nu, nd,
    buf, total, mom, new, in_sem, out_sem, total_sem, mom_sem, new_sem,
):
    count, rows, _ = buf.shape
    per = gin.shape[2] // rows
    ff = total.shape[0] // 3

    def move(n, out):
        b, row = n // per, n % per * rows
        if out:
            return pltpu.make_async_copy(
                buf.at[n], grad_in.at[0, b, pl.ds(row, rows)], out_sem.at[n]
            )
        return pltpu.make_async_copy(gin.at[0, b, pl.ds(row, rows)], buf.at[n], in_sem.at[n])

    moms = [pltpu.make_async_copy(m.at[0], mom.at[n], mom_sem.at[n]) for n, m in enumerate((mg, mu, md))]
    news = [pltpu.make_async_copy(new.at[n], m.at[0], new_sem.at[n]) for n, m in enumerate((ng, nu, nd))]
    totals = pltpu.make_async_copy(total_hbm, total, total_sem)
    for n in range(count):
        move(n, False).start()
    totals.start()
    for copy in moms:
        copy.start()
    for n in range(count):
        move(n, False).wait()
        move(n, True).start()
    totals.wait()
    for n in range(3):
        moms[n].wait()
        new[n] = 0.9 * mom[n] + total[n * ff : (n + 1) * ff, :].T * scale
        news[n].start()
    for copy in news:
        copy.wait()
    for n in range(count):
        move(n, True).wait()


def body(inputs, cotangent, w_gate, w_up, w_down, mom_gate, mom_up, mom_down):
    ns = lax.axis_size("section")
    nz = lax.axis_size("dp") // NH
    _, _, tok, dim = inputs.shape
    ff = w_gate.shape[-1]
    far = nz // 2
    width = dim // (NH * nz)
    cross = int(3 * ff * CROSS) // 32 * 32
    keep = 3 * ff - cross
    anywhere = pl.BlockSpec(memory_space=pl.ANY)
    vmem = pl.BlockSpec(memory_space=pltpu.VMEM)
    dma = pltpu.SemaphoreType.DMA
    gin, total = pl.pallas_call(
        functools.partial(kernel, ns, nz, tok, dim, ff, cross),
        out_shape=(
            jax.ShapeDtypeStruct(inputs.shape, BF16),
            jax.ShapeDtypeStruct((3 * ff, width), F32),
        ),
        in_specs=[anywhere] * 5,
        out_specs=(anywhere, vmem),
        scratch_shapes=[
            pltpu.VMEM((2, tok, dim), BF16),
            pltpu.VMEM((2, tok, dim), BF16),
            pltpu.VMEM((2, dim, ff), BF16),
            pltpu.VMEM((2, dim, ff), BF16),
            pltpu.VMEM((2, ff, dim), BF16),
            pltpu.VMEM((2, 2, tok, ff), BF16),
            pltpu.VMEM((2, 3 * ff, tok), BF16),
            pltpu.VMEM((3, tok, ff), F32),
            pltpu.VMEM((2, NH, nz, keep, width), BF16),
            pltpu.VMEM((2, NH, far, 2, keep, width), BF16),
            pltpu.VMEM((2, tok, dim), BF16),
            pltpu.VMEM((NH + 1, keep, width), BF16),
            pltpu.VMEM((NH + 1, keep, width), BF16),
            pltpu.VMEM((2, NH, nz, cross, width), BF16),
            pltpu.VMEM((NH + 1, nz, cross, width), BF16),
            pltpu.VMEM((2, 2, far, cross // 2, width), BF16),
            dma((2, 5)),
            dma((2, NH, far, 2)),
            dma((2, NH, far, 2)),
            dma((2,)),
            dma((2,)),
            dma,
            dma((NH + 1,)),
            dma((NH + 1,)),
            dma((NH + 1, nz // 2)),
            dma((NH + 1, nz // 2)),
            dma((2, 2, far)),
            dma((2, 2, far)),
        ],
        compiler_params=pltpu.CompilerParams(
            collective_id=0, has_side_effects=True, vmem_limit_bytes=56 * 2**20
        ),
        name="relay_step",
    )(inputs, cotangent, w_gate, w_up, w_down)
    count = 4
    return pl.pallas_call(
        functools.partial(finish_kernel, 1.0 / float(tok * NH * nz) ** 0.5),
        out_shape=(
            jax.ShapeDtypeStruct(inputs.shape, BF16),
            jax.ShapeDtypeStruct(mom_gate.shape, F32),
            jax.ShapeDtypeStruct(mom_up.shape, F32),
            jax.ShapeDtypeStruct(mom_down.shape, F32),
        ),
        in_specs=[anywhere] * 5,
        out_specs=(anywhere,) * 4,
        scratch_shapes=[
            pltpu.VMEM((count, 2 * tok // count, dim), BF16),
            pltpu.VMEM((3 * ff, width), F32),
            pltpu.VMEM((3, width, ff), F32),
            pltpu.VMEM((3, width, ff), F32),
            dma((count,)),
            dma((count,)),
            dma,
            dma((3,)),
            dma((3,)),
        ],
        compiler_params=pltpu.CompilerParams(vmem_limit_bytes=56 * 2**20),
        name="relay_finish",
    )(gin, total, mom_gate, mom_up, mom_down)


def solution(mesh):
    placed = (
        P("section", None, "dp", None),
        P("section", None, "dp", None),
        P("section", None, None, None),
        P("section", None, None, None),
        P("section", None, None, None),
        P("section", "dp", None),
        P("section", "dp", None),
        P("section", "dp", None),
    )
    return jax.shard_map(
        body,
        mesh=mesh,
        in_specs=placed,
        out_specs=(
            P("section", None, "dp", None),
            P("section", "dp", None),
            P("section", "dp", None),
            P("section", "dp", None),
        ),
        check_vma=False,
    )
```

```python
import functools

import jax
import jax.numpy as jnp
from jax import lax
from jax.experimental import pallas as pl
from jax.experimental.pallas import tpu as pltpu
from jax.sharding import PartitionSpec as P

MESH = pl.DeviceIdType.MESH
NH = 2
CROSS = 0.2917
BF16 = jnp.bfloat16
F32 = jnp.float32


def kernel(
    ns, nz, tok, dim, ff, cross,
    x_hbm, y_hbm, wg_hbm, wu_hbm, wd_hbm,
    gin, total_ref,
    xb, yb, wgb, wub, wdb, act, act_t, pre, part, ring, dxb, out1, late,
    wide, wide_in, wide_ring,
    in_sem, ring_send, ring_recv, dx_send, dx_recv, zero_sem, late_send, late_recv,
    wide_send, wide_recv, wide_ring_send, wide_ring_recv,
):
    sec = lax.axis_index("section")
    dp = lax.axis_index("dp")
    half = dp // nz
    z = dp % nz
    width = dim // (NH * nz)
    three = 3 * ff
    keep = three - cross
    far = nz // 2
    pairs = nz // 2
    mirror = ns - 1 - sec

    def at_z(distance):
        return (z + distance + nz) % nz

    def device(s, h, zz):
        return (s, h * nz + zz)

    def start_loads(b):
        for n, (src, dst) in enumerate(
            ((x_hbm, xb), (wg_hbm, wgb), (wu_hbm, wub), (y_hbm, yb), (wd_hbm, wdb))
        ):
            load(b, n, src, dst).start()

    def load(b, n, src, dst):
        return pltpu.make_async_copy(src.at[0, b], dst.at[b], in_sem.at[b, n])

    start_loads(1)

    barrier = pltpu.get_barrier_semaphore()
    neighbours = [
        device(sec, half, at_z(1)),
        device(sec, half, at_z(-1)),
        device(mirror, 0, z),
        device(mirror, 1, z),
        device(sec, 1 - half, z),
        device((sec + 1) % ns, half, z),
        device((sec + ns - 1) % ns, half, z),
    ]
    for target in neighbours:
        pl.semaphore_signal(barrier, inc=1, device_id=target, device_id_type=MESH)

    def forward(i, carry):
        b = 1 - i
        load(b, 0, x_hbm, xb).wait()
        load(b, 1, wg_hbm, wgb).wait()
        if b == 1:
            start_loads(0)
        pre[0] = jnp.dot(xb[b], wgb[b], preferred_element_type=F32)
        load(b, 2, wu_hbm, wub).wait()
        pre[1] = jnp.dot(xb[b], wub[b], preferred_element_type=F32)
        load(b, 3, y_hbm, yb).wait()
        load(b, 4, wd_hbm, wdb).wait()
        pre[2] = lax.dot_general(
            yb[b], wdb[b], (((1,), (1,)), ((), ())), preferred_element_type=F32
        )
        step = min(128, tok)
        for row in range(0, tok, step):
            rows = pl.ds(row, step)
            gpre, upre, dhid = pre[0, rows, :], pre[1, rows, :], pre[2, rows, :]
            sig = jax.nn.sigmoid(gpre)
            activated = gpre * sig
            dgate = dhid * upre * sig * (1.0 + gpre * (1.0 - sig))
            dup = dhid * activated
            hidden = activated * upre
            act[b, 0, rows, :] = dgate.astype(BF16)
            act[b, 1, rows, :] = dup.astype(BF16)
            act_t[b, 0:ff, rows] = dgate.T.astype(BF16)
            act_t[b, ff : 2 * ff, rows] = dup.T.astype(BF16)
            act_t[b, 2 * ff : three, rows] = hidden.T.astype(BF16)
        return carry

    def weight_grad(b, h, pair):
        start = pl.multiple_of((h * nz + 2 * pair) * width, 2 * width)
        cols = pl.ds(start, 2 * width)
        gate_up = jnp.dot(act_t[b, 0 : 2 * ff, :], xb[b, :, cols], preferred_element_type=F32)
        part[b, h, 2 * pair, 0 : 2 * ff, :] = gate_up[:, :width].astype(BF16)
        part[b, h, 2 * pair + 1, 0 : 2 * ff, :] = gate_up[:, width:].astype(BF16)
        down = jnp.dot(act_t[b, 2 * ff : three, :], yb[b, :, cols], preferred_element_type=F32)
        for n in range(2):
            tile = down[:, n * width : (n + 1) * width].astype(BF16)
            if keep > 2 * ff:
                part[b, h, 2 * pair + n, 2 * ff : keep, :] = tile[: keep - 2 * ff]
            wide[b, h, 2 * pair + n] = tile[keep - 2 * ff :]

    def pair_at(piece):
        if pairs == 4:
            piece = (0, 3 - 2 * (z % 2), 1 + 2 * (z % 2), 2)[piece]
        return (z // 2 + far // 2 + piece) % pairs

    def wide_copy(n, piece):
        cols = pl.ds(2 * pair_at(piece), 2)
        if n < NH:
            src, target, slot = wide.at[1, n, cols], device(mirror, n, z), half
        else:
            src, target, slot = wide.at[0, 1 - half, cols], device(sec, 1 - half, z), NH
        return pltpu.make_async_remote_copy(
            src_ref=src,
            dst_ref=wide_in.at[slot, cols],
            send_sem=wide_send.at[n, piece],
            recv_sem=wide_recv.at[slot, piece],
            device_id=target,
            device_id_type=MESH,
        )

    def wide_wait(slot, piece):
        cols = pl.ds(2 * pair_at(piece), 2)
        pltpu.make_async_remote_copy(
            src_ref=wide.at[1, 0, cols],
            dst_ref=wide_in.at[slot, cols],
            send_sem=wide_send.at[0, piece],
            recv_sem=wide_recv.at[slot, piece],
            device_id=device(mirror, 0, z),
            device_id_type=MESH,
        ).wait_recv()

    part_rows = cross // 2

    def wide_message(direction, g, d):
        sign = -1 if direction == 0 else 1
        return pltpu.make_async_remote_copy(
            src_ref=wide.at[0, half, at_z(sign * d), pl.ds(g * part_rows, part_rows)],
            dst_ref=wide_ring.at[direction, g, d - 1],
            send_sem=wide_ring_send.at[direction, g, d - 1],
            recv_sem=wide_ring_recv.at[direction, g, d - 1],
            device_id=device(sec, half, at_z(sign)),
            device_id_type=MESH,
        )

    def wide_sum(target):
        total = wide[0, half, target].astype(F32)
        for slot in range(NH + 1):
            total = total + wide_in[slot, target].astype(F32)
        wide[0, half, target] = total.astype(BF16)

    def wide_accumulate(direction, g, d):
        sign = -1 if direction == 0 else 1
        wide_message(direction, g, d + 1).wait_recv()
        target = at_z(sign * d)
        rows = pl.ds(g * part_rows, part_rows)
        mine = wide[0, half, target, rows, :].astype(F32)
        wide[0, half, target, rows, :] = (mine + wide_ring[direction, g, d].astype(F32)).astype(BF16)

    def message(direction, h, d, b):
        sign = -1 if direction == 0 else 1
        return pltpu.make_async_remote_copy(
            src_ref=part.at[b, h, at_z(sign * d)],
            dst_ref=ring.at[direction, h, d - 1, b],
            send_sem=ring_send.at[direction, h, d - 1, b],
            recv_sem=ring_recv.at[direction, h, d - 1, b],
            device_id=device(sec, half, at_z(sign)),
            device_id_type=MESH,
        )

    def accumulate(direction, h, d, b):
        sign = -1 if direction == 0 else 1
        message(direction, h, d + 1, b).wait_recv()
        target = at_z(sign * d)
        mine = part[b, h, target].astype(F32)
        part[b, h, target] = (mine + ring[direction, h, d, b].astype(F32)).astype(BF16)

    long = ((0, 0), (1, 1))
    short = ((0, 1), (1, 0))

    def dx_copy(b):
        step = -1 if b == 0 else 1
        return pltpu.make_async_remote_copy(
            src_ref=dxb.at[b],
            dst_ref=gin.at[0, b],
            send_sem=dx_send.at[b],
            recv_sem=dx_recv.at[b],
            device_id=device(sec + step, half, z),
            device_id_type=MESH,
        )

    def zero_copy(b):
        return pltpu.make_async_copy(dxb.at[b], gin.at[0, 1 - b], zero_sem)

    cut = 2 * width

    def input_grad(b):
        def dx_chunk(j, carry):
            cols = pl.ds(pl.multiple_of(j * cut, cut), cut)
            contract = (((1,), (1,)), ((), ()))
            dx = lax.dot_general(
                act[b, 0], wgb[b, cols, :], contract, preferred_element_type=F32
            ) + lax.dot_general(act[b, 1], wub[b, cols, :], contract, preferred_element_type=F32)
            dxb[b, :, cols] = dx.astype(BF16)
            return carry

        sends = sec > 0 if b == 0 else sec < ns - 1

        @pl.when(sends)
        def _():
            lax.fori_loop(0, dim // cut, dx_chunk, 0)

        @pl.when(jnp.logical_not(sends))
        def _():
            dxb[b] = jnp.zeros((tok, dim), BF16)
            zero_copy(b).start()

    def send_dx(b):
        @pl.when(sec > 0 if b == 0 else sec < ns - 1)
        def _():
            dx_copy(b).start()

    def ring_step(lanes, d, b):
        for direction, h in lanes:
            accumulate(direction, h, d, b)
            message(direction, h, d, b).start()

    def long_step(d, b):
        ring_step(long, d, b)

    def short_step(d, b):
        if d > 0:
            ring_step(short, d, b)

    def block(b, between):
        forward(1 - b, 0)
        for piece in range(pairs):
            pair = pair_at(piece)
            for h in range(NH):
                weight_grad(b, h, pair)
            if piece == 0:
                if b == 1:
                    pl.semaphore_wait(barrier, len(neighbours))
                for direction, h in long:
                    message(direction, h, far, b).start()
            if piece == 1 and far > 1:
                for direction, h in short:
                    message(direction, h, far - 1, b).start()
            for n in (0, 1) if b == 1 else (NH,):
                wide_copy(n, piece).start()
            between(piece)

    def wide_first():
        for slot in range(NH + 1):
            wide_wait(slot, 0)
        wide_sum(at_z(far))
        for direction, g in long:
            wide_message(direction, g, far).start()

    def wide_second():
        for slot in range(NH + 1):
            wide_wait(slot, 1)
        for sign in (-1, 1):
            wide_sum(at_z(sign * (far - 1)))
        for direction, g in short:
            wide_message(direction, g, far - 1).start()

    def wide_others():
        for piece in range(2, pairs):
            for slot in range(NH + 1):
                wide_wait(slot, piece)
        for d in range(far - 2, -1, -1):
            for sign in (-1, 1) if d > 0 else (1,):
                wide_sum(at_z(sign * d))

    def wide_step(lanes, d):
        for direction, g in lanes:
            wide_accumulate(direction, g, d)
            wide_message(direction, g, d).start()

    if far == 4:
        block(1, lambda piece: None)
        block(0, lambda piece: long_step(3, 1) if piece == 0 else None)
        short_step(2, 1)
        wide_first()
        long_step(3, 0)
        wide_second()
        input_grad(1)
        long_step(2, 1)
        input_grad(0)
        short_step(2, 0)
        wide_others()
        send_dx(1)
        send_dx(0)
        short_step(1, 1)
        long_step(2, 0)
        wide_step(long, 3)
        wide_step(short, 2)
        long_step(1, 1)
        short_step(1, 0)
        wide_step(long, 2)
        wide_step(short, 1)
        long_step(1, 0)
    else:
        block(1, lambda piece: None)
        block(0, lambda piece: None)
        input_grad(1)
        input_grad(0)
        send_dx(1)
        send_dx(0)
        wide_first()
        wide_second()
        wide_others()
        for d in range(far - 1, 0, -1):
            for b in (1, 0):
                long_step(d, b)
                short_step(d - 1, b)
            if d > 1:
                wide_step(long, d)
                if d > 2:
                    wide_step(short, d - 1)

    def reduced(b, h):
        return (
            part[b, h, z].astype(F32)
            + ring[0, h, 0, b].astype(F32)
            + ring[1, h, 0, b].astype(F32)
        )

    def finish_wait(b, h):
        message(0, h, 1, b).wait_recv()
        message(1, h, 1, b).wait_recv()

    def late_copy(n):
        if n < NH:
            target, slot = device(mirror, n, z), half
        else:
            target, slot = device(sec, 1 - half, z), NH
        return pltpu.make_async_remote_copy(
            src_ref=out1.at[n],
            dst_ref=late.at[slot],
            send_sem=late_send.at[n],
            recv_sem=late_recv.at[slot],
            device_id=target,
            device_id_type=MESH,
        )

    for h in range(NH):
        finish_wait(1, h)
        out1[h] = reduced(1, h).astype(BF16)
        late_copy(h).start()
    for h in range(NH):
        finish_wait(0, h)
    out1[NH] = reduced(0, 1 - half).astype(BF16)
    late_copy(NH).start()

    wide_step(long, 1)

    def late_wait(slot):
        pltpu.make_async_remote_copy(
            src_ref=out1.at[0],
            dst_ref=late.at[slot],
            send_sem=late_send.at[0],
            recv_sem=late_recv.at[slot],
            device_id=device(mirror, 0, z),
            device_id_type=MESH,
        ).wait_recv()

    for slot in range(3):
        late_wait(slot)
    for direction in range(2):
        for g in range(2):
            wide_message(direction, g, 1).wait_recv()

    def total_of(lo, hi):
        rows = pl.ds(lo, hi - lo)
        total = (
            part[0, half, z, rows, :].astype(F32)
            + ring[0, half, 0, 0, rows, :].astype(F32)
            + ring[1, half, 0, 0, rows, :].astype(F32)
        )
        for slot in range(3):
            total = total + late[slot, rows, :].astype(F32)
        return total

    pieces = [total_of(2 * ff, keep)] if keep > 2 * ff else []
    for g in range(2):
        rows = pl.ds(g * part_rows, part_rows)
        pieces.append(
            wide[0, half, z, rows, :].astype(F32)
            + wide_ring[0, g, 0].astype(F32)
            + wide_ring[1, g, 0].astype(F32)
        )
    total_ref[0:ff, :] = total_of(0, ff)
    total_ref[ff : 2 * ff, :] = total_of(ff, 2 * ff)
    total_ref[2 * ff : three, :] = jnp.concatenate(pieces, axis=0)

    for h in range(NH):
        late_copy(h).wait_send()
    late_copy(NH).wait_send()
    for n in range(NH + 1):
        for piece in range(pairs):
            wide_copy(n, piece).wait_send()
    for d in range(1, far + 1):
        for direction, g in long + (short if d < far else ()):
            wide_message(direction, g, d).wait_send()
    for b in range(2):
        for d in range(1, far + 1):
            for direction, h in long + (short if d < far else ()):
                message(direction, h, d, b).wait_send()

    @pl.when(sec > 0)
    def _():
        dx_copy(0).wait_send()
        dx_copy(1).wait_recv()

    @pl.when(sec < ns - 1)
    def _():
        dx_copy(1).wait_send()
        dx_copy(0).wait_recv()

    @pl.when(sec == 0)
    def _():
        zero_copy(0).wait()

    @pl.when(sec == ns - 1)
    def _():
        zero_copy(1).wait()


def finish_kernel(
    scale, gin, total_hbm, mg, mu, md, grad_in, ng, nu, nd,
    buf, total, mom, new, in_sem, out_sem, total_sem, mom_sem, new_sem,
):
    count, rows, _ = buf.shape
    per = gin.shape[2] // rows
    ff = total.shape[0] // 3

    def move(n, out):
        b, row = n // per, n % per * rows
        if out:
            return pltpu.make_async_copy(
                buf.at[n], grad_in.at[0, b, pl.ds(row, rows)], out_sem.at[n]
            )
        return pltpu.make_async_copy(gin.at[0, b, pl.ds(row, rows)], buf.at[n], in_sem.at[n])

    moms = [pltpu.make_async_copy(m.at[0], mom.at[n], mom_sem.at[n]) for n, m in enumerate((mg, mu, md))]
    news = [pltpu.make_async_copy(new.at[n], m.at[0], new_sem.at[n]) for n, m in enumerate((ng, nu, nd))]
    totals = pltpu.make_async_copy(total_hbm, total, total_sem)
    for n in range(count):
        move(n, False).start()
    totals.start()
    for copy in moms:
        copy.start()
    for n in range(count):
        move(n, False).wait()
        move(n, True).start()
    totals.wait()
    for n in range(3):
        moms[n].wait()
        new[n] = 0.9 * mom[n] + total[n * ff : (n + 1) * ff, :].T * scale
        news[n].start()
    for copy in news:
        copy.wait()
    for n in range(count):
        move(n, True).wait()


def body(inputs, cotangent, w_gate, w_up, w_down, mom_gate, mom_up, mom_down):
    ns = lax.axis_size("section")
    nz = lax.axis_size("dp") // NH
    _, _, tok, dim = inputs.shape
    ff = w_gate.shape[-1]
    far = nz // 2
    width = dim // (NH * nz)
    cross = int(3 * ff * CROSS) // 32 * 32
    keep = 3 * ff - cross
    anywhere = pl.BlockSpec(memory_space=pl.ANY)
    vmem = pl.BlockSpec(memory_space=pltpu.VMEM)
    dma = pltpu.SemaphoreType.DMA
    gin, total = pl.pallas_call(
        functools.partial(kernel, ns, nz, tok, dim, ff, cross),
        out_shape=(
            jax.ShapeDtypeStruct(inputs.shape, BF16),
            jax.ShapeDtypeStruct((3 * ff, width), F32),
        ),
        in_specs=[anywhere] * 5,
        out_specs=(anywhere, vmem),
        scratch_shapes=[
            pltpu.VMEM((2, tok, dim), BF16),
            pltpu.VMEM((2, tok, dim), BF16),
            pltpu.VMEM((2, dim, ff), BF16),
            pltpu.VMEM((2, dim, ff), BF16),
            pltpu.VMEM((2, ff, dim), BF16),
            pltpu.VMEM((2, 2, tok, ff), BF16),
            pltpu.VMEM((2, 3 * ff, tok), BF16),
            pltpu.VMEM((3, tok, ff), F32),
            pltpu.VMEM((2, NH, nz, keep, width), BF16),
            pltpu.VMEM((2, NH, far, 2, keep, width), BF16),
            pltpu.VMEM((2, tok, dim), BF16),
            pltpu.VMEM((NH + 1, keep, width), BF16),
            pltpu.VMEM((NH + 1, keep, width), BF16),
            pltpu.VMEM((2, NH, nz, cross, width), BF16),
            pltpu.VMEM((NH + 1, nz, cross, width), BF16),
            pltpu.VMEM((2, 2, far, cross // 2, width), BF16),
            dma((2, 5)),
            dma((2, NH, far, 2)),
            dma((2, NH, far, 2)),
            dma((2,)),
            dma((2,)),
            dma,
            dma((NH + 1,)),
            dma((NH + 1,)),
            dma((NH + 1, nz // 2)),
            dma((NH + 1, nz // 2)),
            dma((2, 2, far)),
            dma((2, 2, far)),
        ],
        compiler_params=pltpu.CompilerParams(
            collective_id=0, has_side_effects=True, vmem_limit_bytes=56 * 2**20
        ),
        name="relay_step",
    )(inputs, cotangent, w_gate, w_up, w_down)
    count = 4
    return pl.pallas_call(
        functools.partial(finish_kernel, 1.0 / float(tok * NH * nz) ** 0.5),
        out_shape=(
            jax.ShapeDtypeStruct(inputs.shape, BF16),
            jax.ShapeDtypeStruct(mom_gate.shape, F32),
            jax.ShapeDtypeStruct(mom_up.shape, F32),
            jax.ShapeDtypeStruct(mom_down.shape, F32),
        ),
        in_specs=[anywhere] * 5,
        out_specs=(anywhere,) * 4,
        scratch_shapes=[
            pltpu.VMEM((count, 2 * tok // count, dim), BF16),
            pltpu.VMEM((3 * ff, width), F32),
            pltpu.VMEM((3, width, ff), F32),
            pltpu.VMEM((3, width, ff), F32),
            dma((count,)),
            dma((count,)),
            dma,
            dma((3,)),
            dma((3,)),
        ],
        compiler_params=pltpu.CompilerParams(vmem_limit_bytes=56 * 2**20),
        name="relay_finish",
    )(gin, total, mom_gate, mom_up, mom_down)


def solution(mesh):
    placed = (
        P("section", None, "dp", None),
        P("section", None, "dp", None),
        P("section", None, None, None),
        P("section", None, None, None),
        P("section", None, None, None),
        P("section", "dp", None),
        P("section", "dp", None),
        P("section", "dp", None),
    )
    return jax.shard_map(
        body,
        mesh=mesh,
        in_specs=placed,
        out_specs=(
            P("section", None, "dp", None),
            P("section", "dp", None),
            P("section", "dp", None),
            P("section", "dp", None),
        ),
        check_vma=False,
    )
```
